512 devices in a mesh: prow: 32 (over x, z), pcol: 16 (over y, core).
Axes of the slice: x: 4, y: 8, z: 8, core: 2. Of those that a mesh axis runs over, the one named last changes fastest.
Arguments:
- pool_inverse: float32 [8192, 8192], P('prow', 'pcol'), may hold values from -6 to 6
- panel_blocks: float32 [1, 8192, 512], P(None, 'prow'), may hold values from -0.09375 to 0.09375
- prev_panel: float32 [1, 512, 512], P(None, 'prow'), may hold values from -0.25 to 0.25
- pivot_inverse: float32 [1, 512, 512], P(None, 'pcol'), may hold values from -6 to 6
- top_column: float32 [512, 8192], P('pcol', 'prow'), may hold values from -6 to 6
- top_diag: float32 [512, 512], P('pcol'), may hold values from -6 to 6
- slot_blocks: int32 [1, 64], replicated, may hold values from -1 to 63, as said below
Outputs:
- column_out: float32 [1, 512, 8192], P(None, 'pcol', 'prow')
- cross_out: float32 [1, 512, 512], P(None, 'pcol')
- diag_out: float32 [1, 512, 512], P(None, 'pcol')
The draws below stay inside these ranges and needn't reach their ends.
Inputs may be any that keep to these rules, and one draw needn't show every extreme that they name: `slot_blocks`: row owner r's slots, entries r * 2 to r * 2 + 1 of a supernode's list, name distinct pool blocks of r * 2 to r * 2 + 1 in ascending order, followed by -1 for unused slots. In every supernode the 2 row owners of some aligned group of 2 use all their slots.
All inputs are finite; a program needn't handle non-finite values.
Results may differ from the reference program's by a relative error of at most 0.0001.
Values sent between devices are 32-bit elements; how exact they have to be, the bound alone decides.
No kernel may reach another device: no remote copies, remote signals or barrier semaphores. Data moves between devices by JAX's collectives and lax.ppermute only.
A program may use at most 64 MiB of HBM per device.

```python
import jax
import jax.numpy as jnp
from jax import lax

W = 512
BLK = 128
SLOTS = 2
SN = 1
RBLK = 2
QGRP = 2
NA = 64
M = 8192
PANEL = 8192
N_PROW = 32


def draw_slot_blocks(key, part):
    key_count, key_group, key_order = jax.random.split(jax.random.fold_in(key, 17), 3)
    owners = jnp.arange(N_PROW, dtype=jnp.int32)
    supernodes = jnp.arange(SN, dtype=jnp.int32)
    counts = jax.random.randint(key_count, (SN, N_PROW), 0, SLOTS + 1)
    group_start = jax.random.randint(key_group, (SN, 1), 0, N_PROW // QGRP) * QGRP
    whole_group = (owners[None, :] >= group_start) & (owners[None, :] < group_start + QGRP)
    short_owner = (owners[None, :] == (group_start + QGRP) % N_PROW) & (supernodes[:, None] >= 1)
    top_owner = (owners[None, :] == N_PROW - 1) & (supernodes[:, None] == 0)
    counts = jnp.where(whole_group | top_owner, SLOTS, counts)
    counts = jnp.where(short_owner, SLOTS - 1, counts)
    scores = jax.random.randint(key_order, (SN, N_PROW, RBLK), 0, 1 << 20) * RBLK + jnp.arange(RBLK, dtype=jnp.int32)
    lifted = top_owner[:, :, None] & (jnp.arange(RBLK) == RBLK - 1)[None, None, :]
    scores = jnp.where(lifted, -1, scores)
    chosen = jnp.sort(jnp.argsort(scores, axis=2)[:, :, :SLOTS], axis=2).astype(jnp.int32)
    blocks_global = owners[None, :, None] * RBLK + chosen
    slot_ids = jnp.where(jnp.arange(SLOTS)[None, None, :] < counts[:, :, None], blocks_global, -1)
    return slot_ids.reshape(SN, N_PROW * SLOTS).astype(jnp.int32)


def levels(key, extent, cuts, least, top_value):
    loudness = 1.0
    for dim, shards_of in cuts:
        steps = jax.random.uniform(jax.random.fold_in(jax.random.fold_in(key, 6), dim), (shards_of,), jnp.float32, least / len(cuts), top_value / len(cuts))
        loudness = loudness * jnp.repeat(jnp.exp(steps), extent[dim] // shards_of).reshape((-1,) + (1,) * (len(extent) - 1 - dim))
    return loudness


def centred(own_key, dims, scale, most, cuts=(), held_as=jnp.bfloat16):
    loudness = levels(own_key, dims, cuts, -0.22, 0.18) if cuts else 1.0
    result = jax.random.normal(own_key, dims, jnp.float32) * scale * loudness
    return jnp.minimum(jnp.maximum(result, -most), most).astype(held_as)


def setup_inputs(seed: int = 0) -> dict:
    splits = jax.random.split(jax.random.key(seed), 8)
    return {
        "pool_inverse": centred(splits[0], (M, M), 1.0, 6.0, ((0, 32), (1, 16)), jnp.float32),
        "panel_blocks": centred(splits[1], (SN, PANEL, W), (N_PROW * BLK) ** -0.5, 0.09375, ((1, 32),), jnp.float32),
        "prev_panel": centred(splits[2], (SN, W, W), W ** -0.5, 0.25, ((1, 32),), jnp.float32),
        "pivot_inverse": centred(splits[3], (SN, W, W), 1.0, 6.0, ((1, 16),), jnp.float32),
        "top_column": centred(splits[4], (W, M), 1.0, 6.0, ((0, 16), (1, 32)), jnp.float32),
        "top_diag": centred(splits[5], (W, W), 1.0, 6.0, ((0, 16),), jnp.float32),
        "slot_blocks": draw_slot_blocks(jax.random.fold_in(splits[7], 71), 0),
    }


highest = lax.Precision.HIGHEST


def matmul(left, right):
    return jnp.dot(left, right, precision=highest, preferred_element_type=jnp.float32)


def reference(pool_inverse, panel_blocks, prev_panel, pivot_inverse, top_column, top_diag, slot_blocks):
    chain_column = top_column
    chain_diag = top_diag
    columns_out = []
    cross_out = []
    diag_out = []
    for supernode in range(SN):
        slot_ids = slot_blocks[supernode]
        usable = slot_ids >= 0
        target = jnp.where(usable, slot_ids, 0).astype(jnp.int32)
        pieces = panel_blocks[supernode].reshape(N_PROW * SLOTS, BLK, W) * usable.astype(jnp.float32)[:, None, None]
        factor_rows = jnp.zeros((NA, BLK, W), jnp.float32).at[target].add(pieces).reshape(NA * BLK, W)
        factor_prev = prev_panel[supernode]
        combined = matmul(pool_inverse, factor_rows) + matmul(chain_column.T, factor_prev)
        fresh_column = -combined.T
        cross_block = -(matmul(chain_column, factor_rows) + matmul(chain_diag, factor_prev))
        diag_block = pivot_inverse[supernode] - (matmul(fresh_column, factor_rows) + matmul(cross_block.T, factor_prev))
        columns_out.append(fresh_column)
        cross_out.append(cross_block)
        diag_out.append(diag_block)
        chain_column = fresh_column
        chain_diag = diag_block
    return jnp.stack(columns_out), jnp.stack(cross_out), jnp.stack(diag_out)
```

```python
import jax
import jax.numpy as jnp
from jax import lax
from jax.sharding import PartitionSpec as P

BLK = 128
ROWS = 32
COLS = 16
YS = 8

highest = lax.Precision.HIGHEST


def matmul(left, right):
    return jnp.dot(left, right, precision=highest, preferred_element_type=jnp.float32)


def contract(left, right, ldim, rdim):
    return lax.dot_general(
        left, right, (((ldim,), (rdim,)), ((), ())), precision=highest, preferred_element_type=jnp.float32
    )


def spread_pairs():
    pairs = []
    for row in range(ROWS):
        for col in range(COLS):
            y, q, z = row // 4, row % 4, row % 8
            t = (col // 2 - y - 4 + z) % 8
            pairs.append((row * COLS + col, (8 * q + t) * COLS + 2 * y + col % 2))
    return pairs


def body(pool_inverse, panel_blocks, prev_panel, pivot_inverse, top_column, top_diag, slot_blocks):
    row = lax.axis_index("prow")
    col = lax.axis_index("pcol")
    y = col // 2
    core = col % 2
    partner = [(i, i ^ 1) for i in range(COLS)]

    ids = lax.dynamic_slice_in_dim(slot_blocks[0], row * 2, 2)
    first, second = panel_blocks[0, :BLK], panel_blocks[0, BLK:]
    zero = jnp.zeros_like(first)
    factor = jnp.concatenate(
        [
            jnp.where(ids[0] == 2 * row, first, zero),
            jnp.where(ids[0] == 2 * row + 1, first, jnp.where(ids[1] == 2 * row + 1, second, zero)),
        ],
        0,
    )
    prev = prev_panel[0]

    def split_cols(value):
        return value.reshape(value.shape[0], YS, 2, 32)

    def pick_core(value, which):
        return lax.dynamic_index_in_dim(split_cols(value), which, 2, keepdims=False).reshape(value.shape[0], 256)

    piece = (y - row // 4 - 4 + row % 8) % 8
    own_piece = jnp.concatenate(
        [
            lax.dynamic_slice_in_dim(factor, 32 * piece, 32, 0),
            lax.dynamic_slice_in_dim(prev, 2 * piece, 2, 0),
            jnp.zeros((6, 512), jnp.float32),
        ],
        0,
    )
    spread = lax.ppermute(pick_core(own_piece, core), ("prow", "pcol"), spread_pairs())
    pool_other = lax.ppermute(pool_inverse, "pcol", partner)

    diag_slice = lax.dynamic_slice_in_dim(top_diag, row * 16, 16, 1)
    cross_part = matmul(top_column, factor) + matmul(diag_slice, prev)
    swapped = lax.ppermute(
        jnp.concatenate([top_column, pick_core(cross_part, 1 - core)], 1), "pcol", partner
    )
    column_other = swapped[:, :256]
    cross_own = pick_core(cross_part, core)
    cross_other = swapped[:, 256:]
    cross_pair = jnp.where(
        core == 0, jnp.stack([cross_own, cross_other], 1), jnp.stack([cross_other, cross_own], 1)
    )
    prev_rows = prev.reshape(16, 2, 256)
    extra = jnp.concatenate(
        [cross_pair, jnp.concatenate([prev_rows, prev_rows], 0), cross_part.reshape(32, 2, 256)], 1
    )
    send = jnp.concatenate([jnp.broadcast_to(spread[None, :34], (ROWS, 34, 256)), extra], 1)
    got = lax.all_to_all(send, "prow", 0, 0, tiled=True)

    rows_all = got[:, :32].reshape(1024, 256)
    prev_all = got[:, 32:34].reshape(64, 256)
    cross_rows = -jnp.sum(got[:, 34:36], 0)
    prev_stride = lax.dynamic_index_in_dim(
        got.reshape(16, 2, 40, 256)[:, :, 36:38], row // 16, 1, keepdims=False
    ).reshape(16, 512)
    cross_full = -jnp.sum(got[:, 38:40], 0)

    own_rows = lax.dynamic_slice_in_dim(rows_all, 512 * core, 512, 0)
    other_rows = lax.dynamic_slice_in_dim(rows_all, 512 * (1 - core), 512, 0)
    own_prev = lax.dynamic_slice_in_dim(prev_all, 32 * core, 32, 0)
    other_prev = lax.dynamic_slice_in_dim(prev_all, 32 * (1 - core), 32, 0)
    part = (
        contract(own_rows, pool_inverse, 0, 1)
        + contract(other_rows, pool_other, 0, 1)
        + contract(own_prev, top_column, 0, 0)
        + contract(other_prev, column_other, 0, 0)
    )
    cross_send = cross_rows.reshape(2, YS, 32).transpose(1, 0, 2).reshape(YS, 1, 64)
    send = jnp.concatenate(
        [part.reshape(YS, 32, 256), jnp.pad(cross_send, ((0, 0), (0, 7), (0, 192)))], 1
    )
    groups = [[2 * i + k for i in range(YS)] for k in range(2)]
    got = lax.all_to_all(send, "pcol", 0, 0, tiled=True, axis_index_groups=groups)
    fresh = -jnp.sum(got[:, :32], 0)
    cross_cols = got[:, 32, :64].reshape(16, 32)

    diag_part = matmul(fresh, factor) + contract(cross_cols, prev_stride, 0, 0)
    send = jnp.concatenate(
        [
            diag_part.reshape(ROWS, 4, 128),
            jnp.broadcast_to(cross_full.reshape(1, 4, 128), (ROWS, 4, 128)),
        ],
        1,
    )
    got = lax.all_to_all(send, "prow", 0, 0, tiled=True)
    cross_out = got[:, 4:].reshape(1, 32, 512)
    total = jnp.sum(got[:, :4], 0)
    got = lax.all_to_all(jnp.broadcast_to(total, (ROWS, 4, 128)), "prow", 0, 0, tiled=True)
    diag_out = pivot_inverse - got.reshape(1, 32, 512)
    return fresh[None], cross_out, diag_out


def solution(mesh):
    in_specs = (
        P("prow", "pcol"),
        P(None, "prow", None),
        P(None, "prow", None),
        P(None, "pcol", None),
        P("pcol", "prow"),
        P("pcol", None),
        P(),
    )
    out_specs = (P(None, "pcol", "prow"), P(None, "pcol", None), P(None, "pcol", None))
    return jax.shard_map(body, mesh=mesh, in_specs=in_specs, out_specs=out_specs, check_vma=False)
```

```python
import jax
import jax.numpy as jnp
from jax import lax
from jax.experimental import pallas as pl
from jax.experimental.pallas import tpu as pltpu
from jax.sharding import PartitionSpec as P


BLK = 128
ROWS = 32
COLS = 16
YS = 8

highest = lax.Precision.HIGHEST
kernel_params = pltpu.CompilerParams(vmem_limit_bytes=16 << 20)


def matmul(left, right):
    return jnp.dot(left, right, precision=highest, preferred_element_type=jnp.float32)


def spread_pairs():
    pairs = []
    for row in range(ROWS):
        for col in range(COLS):
            y, q, z = row // 4, row % 4, row % 8
            t = (col // 2 - y - 4 + z) % 8
            pairs.append((row * COLS + col, (8 * q + t) * COLS + 2 * y + col % 2))
    return pairs


def select_columns(core):
    source = lax.broadcasted_iota(jnp.int32, (512, 256), 0)
    n = lax.broadcasted_iota(jnp.int32, (512, 256), 1)
    wanted = 64 * ((n % 128) // 16) + 32 * core + 16 * (n // 128) + n % 16
    return (source == wanted).astype(jnp.float32)


def dot(left, right):
    return jnp.dot(left, right, precision=highest, preferred_element_type=jnp.float32)


def piece_kernel(slots, panel, prev, out, buffer, sems):
    row = lax.axis_index("prow")
    col = lax.axis_index("pcol")
    piece = (col // 2 + 16 - row // 4 - 4 + row % 8) % 8
    offset = 32 * (piece % 4)
    copies = [
        pltpu.make_async_copy(panel.at[0, pl.ds(BLK * k + offset, 32), :], buffer.at[k], sems.at[k]) for k in range(2)
    ]
    for copy in copies:
        copy.start()
    wanted = 2 * row + piece // 4
    rolled = pltpu.roll(prev[0], (16 - 2 * piece) % 16, 0)
    columns = select_columns(col % 2)
    for copy in copies:
        copy.wait()
    zero = jnp.zeros((32, 512), jnp.float32)
    chunk = jnp.where(slots[0, 2 * row] == wanted, buffer[0], zero)
    chunk = jnp.where(slots[0, 2 * row + 1] == wanted, buffer[1], chunk)
    out[...] = dot(jnp.concatenate([chunk, rolled[:8]], 0), columns)


def own_piece(slot_blocks, panel_blocks, prev_panel):
    return pl.pallas_call(
        piece_kernel,
        out_shape=jax.ShapeDtypeStruct((40, 256), jnp.float32),
        in_specs=[
            pl.BlockSpec(memory_space=pltpu.SMEM),
            pl.BlockSpec(memory_space=pl.ANY),
            pl.BlockSpec(memory_space=pltpu.VMEM),
        ],
        out_specs=pl.BlockSpec(memory_space=pltpu.VMEM),
        scratch_shapes=[pltpu.VMEM((2, 32, 512), jnp.float32), pltpu.SemaphoreType.DMA((2,))],
        compiler_params=kernel_params,
        name="own_piece",
    )(slot_blocks, panel_blocks, prev_panel)


def gather_kernel(spread, cross_own, cross_other, cross_part, prev, out):
    core = lax.axis_index("pcol") % 2
    for k in range(ROWS):
        out[k, :40, :] = spread[:, 128 * (k % 2) : 128 * (k % 2) + 128]
        out[k, 40:, :] = jnp.zeros((8, 128), jnp.float32)
    mine, others = cross_own[...], cross_other[...]
    pair = [jnp.where(core == 0, mine, others), jnp.where(core == 0, others, mine)]
    part = cross_part[...]
    for k in range(ROWS):
        for lane in range(2):
            for who in range(2):
                at = 34 + 2 * who + lane
                out[k, at : at + 1, :] = pair[who][k : k + 1, 128 * lane : 128 * lane + 128]
        for lane in range(4):
            span = slice(128 * lane, 128 * lane + 128)
            out[k, 38 + lane : 39 + lane, :] = prev[0, k % 16 : k % 16 + 1, span]
            out[k, 42 + lane : 43 + lane, :] = part[k : k + 1, span]


def gather_operand(spread, cross_own, cross_other, cross_part, prev_panel):
    return pl.pallas_call(
        gather_kernel,
        out_shape=jax.ShapeDtypeStruct((ROWS, 48, 128), jnp.float32),
        in_specs=[pl.BlockSpec(memory_space=pltpu.VMEM)] * 5,
        out_specs=pl.BlockSpec(memory_space=pltpu.VMEM),
        compiler_params=kernel_params,
        name="gather_operand",
    )(spread, cross_own, cross_other, cross_part, prev_panel)


def product_kernel(got, mine, mine_b, next_z, next_zb, out, cross_full, stride, prev_rows):
    row = lax.axis_index("prow")
    core = lax.axis_index("pcol") % 2
    half = row % 2
    for k in range(ROWS):
        prev_rows[2 * k : 2 * k + 2, :] = got[k, 32:34, :]
    own = got[pl.ds(16 * core, 16), :32, :].reshape(512, 128)
    other = got[pl.ds(16 - 16 * core, 16), :32, :].reshape(512, 128)
    own_prev = prev_rows[pl.ds(pl.multiple_of(32 * core, 32), 32), :]
    other_prev = prev_rows[pl.ds(pl.multiple_of(32 - 32 * core, 32), 32), :]
    prev = jnp.concatenate([own_prev, other_prev], 0)
    sums = -jnp.sum(got[:, 32:48, :], 0)
    cross = jnp.concatenate([sums[2:6], jnp.zeros((4, 128), jnp.float32)], 0)
    cross = jnp.concatenate([cross, jnp.zeros((8, 128), jnp.float32)], 1)
    cross_full[...] = sums[10:14]
    for c in range(COLS):
        stride[4 * c : 4 * c + 4, :] = got[2 * c + row // 16, 38:42, :]
    for left, right, which in ((mine, mine_b, half), (next_z, next_zb, 1 - half)):
        top = jnp.concatenate([left[256:, :256], left[256:, 256:], right[256:, :256], right[256:, 256:]], 0)
        part = dot(left[:256, :], own) + dot(right[:256, :], other) + dot(top.T, prev)
        part = part.T
        for y in range(YS):
            out[2 * y + which, :16, :] = part[16 * y : 16 * y + 16, :]
            out[2 * y + which, 16:, :] = cross


def column_product(got, mine, mine_b, next_z, next_zb):
    return pl.pallas_call(
        product_kernel,
        out_shape=(
            jax.ShapeDtypeStruct((16, 24, 256), jnp.float32),
            jax.ShapeDtypeStruct((4, 128), jnp.float32),
            jax.ShapeDtypeStruct((64, 128), jnp.float32),
        ),
        in_specs=[pl.BlockSpec(memory_space=pltpu.VMEM)] * 5,
        out_specs=(pl.BlockSpec(memory_space=pltpu.VMEM),) * 3,
        scratch_shapes=[pltpu.VMEM((64, 128), jnp.float32)],
        compiler_params=kernel_params,
        name="column_product",
    )(got, mine, mine_b, next_z, next_zb)


def diag_kernel(got, factor, cross_full, stride, fresh_out, out, columns):
    half = lax.axis_index("prow") % 2
    y = lax.axis_index("pcol") // 2
    fresh = []
    for h in range(2):
        total = got[h, :16, :]
        for k in range(1, YS):
            total = total + got[2 * k + h, :16, :]
        fresh.append(-total)
    fresh = jnp.concatenate(fresh, 0)
    fresh_out[0] = fresh
    part = dot(fresh, factor[...])
    for k in range(YS):
        block = got[2 * k + half, 16:24, :128]
        for who in range(2):
            for h in range(2):
                columns[h, 2 * k + who : 2 * k + who + 1, :] = block[2 * who + h : 2 * who + h + 1]
    rows = jnp.concatenate([stride[pl.ds(lane, 16, stride=4), :] for lane in range(4)], 1)
    own = []
    for h in range(2):
        columns[2 + h, :, :] = jnp.zeros((128, 128), jnp.float32)
        columns[2 + h, :, :16] = columns[h, :16, :].T
        picked = columns[2 + h, pl.ds(pl.multiple_of(16 * y, 16), 16), :]
        own.append(dot(picked[:, :16], rows))
    part = part + jnp.concatenate(own, 0)
    for k in range(ROWS):
        for lane in range(4):
            out[k, lane : lane + 1, :] = part[k : k + 1, 128 * lane : 128 * lane + 128]
        out[k, 4:8, :] = cross_full[...]


def diag_operand(got, factor, cross_full, stride):
    return pl.pallas_call(
        diag_kernel,
        out_shape=(
            jax.ShapeDtypeStruct((1, 32, 256), jnp.float32),
            jax.ShapeDtypeStruct((ROWS, 8, 128), jnp.float32),
        ),
        in_specs=[pl.BlockSpec(memory_space=pltpu.VMEM)] * 4,
        out_specs=(pl.BlockSpec(memory_space=pltpu.VMEM),) * 2,
        scratch_shapes=[pltpu.VMEM((4, 128, 128), jnp.float32)],
        compiler_params=kernel_params,
        name="diag_operand",
    )(got, factor, cross_full, stride)


def step(pool_inverse, panel_blocks, prev_panel, pivot_inverse, top_column, top_diag, slot_blocks):
    row = lax.axis_index("prow")
    core = lax.axis_index("pcol") % 2
    core_swap = [(i, i ^ 1) for i in range(COLS)]
    row_swap = [(i, i ^ 1) for i in range(ROWS)]

    sent = own_piece(slot_blocks, panel_blocks, prev_panel)
    sent, top_column, top_diag = lax.optimization_barrier((sent, top_column, top_diag))
    spread = lax.ppermute(sent, ("prow", "pcol"), spread_pairs())

    blocks = jnp.concatenate([pool_inverse, jnp.concatenate([top_column[:16], top_column[16:]], 1)], 0)
    blocks_z = lax.ppermute(blocks, "prow", row_swap)
    blocks_b = lax.ppermute(blocks, "pcol", core_swap)

    ids = lax.dynamic_slice_in_dim(slot_blocks[0], row * 2, 2)
    first, second = panel_blocks[0, :BLK], panel_blocks[0, BLK:]
    zero = jnp.zeros_like(first)
    factor = jnp.concatenate(
        [
            jnp.where(ids[0] == 2 * row, first, zero),
            jnp.where(ids[0] == 2 * row + 1, first, jnp.where(ids[1] == 2 * row + 1, second, zero)),
        ],
        0,
    )
    diag_slice = lax.dynamic_slice_in_dim(top_diag, row * 16, 16, 1)
    cross_part = matmul(top_column, factor) + matmul(diag_slice, prev_panel[0])
    cross_sent = matmul(cross_part, select_columns(1 - core))
    cross_own = matmul(cross_part, select_columns(core))
    cross_other = lax.ppermute(cross_sent, "pcol", core_swap)

    spread, blocks_z, blocks_b, cross_other = lax.optimization_barrier((spread, blocks_z, blocks_b, cross_other))
    send = gather_operand(spread, cross_own, cross_other, cross_part, prev_panel)
    got = lax.all_to_all(send, "prow", 0, 0, tiled=True)
    blocks_zb = lax.ppermute(blocks_z, "pcol", core_swap)

    send, cross_full, stride = column_product(got, blocks, blocks_b, blocks_z, blocks_zb)
    groups = [
        [(x * 8 + 2 * z + h) * COLS + 2 * i + k for i in range(YS) for h in range(2)]
        for x in range(4)
        for z in range(4)
        for k in range(2)
    ]
    got = lax.all_to_all(send, ("prow", "pcol"), 0, 0, tiled=True, axis_index_groups=groups)
    fresh, send = diag_operand(got, factor, cross_full, stride)
    got = lax.all_to_all(send, "prow", 0, 0, tiled=True)
    cross_out = got[:, 4:].reshape(1, 32, 512)
    total = jnp.sum(got[:, :4], 0)
    got = lax.all_to_all(jnp.broadcast_to(total, (ROWS, 4, 128)), "prow", 0, 0, tiled=True)
    diag_out = pivot_inverse - got.reshape(1, 32, 512)
    return fresh, cross_out, diag_out


def solution(mesh):
    in_specs = (
        P("prow", "pcol"),
        P(None, "prow", None),
        P(None, "prow", None),
        P(None, "pcol", None),
        P("pcol", "prow"),
        P("pcol", None),
        P(),
    )
    out_specs = (P(None, "pcol", "prow"), P(None, "pcol", None), P(None, "pcol", None))
    return jax.shard_map(step, mesh=mesh, in_specs=in_specs, out_specs=out_specs, check_vma=False)
```

```python
import jax
import jax.numpy as jnp
from jax import lax
from jax.experimental import pallas as pl
from jax.experimental.pallas import tpu as pltpu
from jax.sharding import PartitionSpec as P


BLK = 128
ROWS = 32
COLS = 16
YS = 8

highest = lax.Precision.HIGHEST
kernel_params = pltpu.CompilerParams(vmem_limit_bytes=16 << 20)


def spread_pairs():
    pairs = []
    for row in range(ROWS):
        for col in range(COLS):
            y, q, z = row // 4, row % 4, row % 8
            t = (col // 2 - y - 4 + z) % 8
            pairs.append((row * COLS + col, (8 * q + t) * COLS + 2 * y + col % 2))
    return pairs


def select_columns(core):
    source = lax.broadcasted_iota(jnp.int32, (512, 256), 0)
    n = lax.broadcasted_iota(jnp.int32, (512, 256), 1)
    wanted = 64 * ((n % 128) // 16) + 32 * core + 16 * (n // 128) + n % 16
    return (source == wanted).astype(jnp.float32)


def dot(left, right):
    return jnp.dot(left, right, precision=highest, preferred_element_type=jnp.float32)


def piece_kernel(slots, panel, prev, out, ids, buffer, rows, sems):
    row = lax.axis_index("prow")
    col = lax.axis_index("pcol")
    piece = (col // 2 + 16 - row // 4 - 4 + row % 8) % 8
    offset = 32 * (piece % 4)
    copies = [
        pltpu.make_async_copy(panel.at[0, pl.ds(BLK * k + offset, 32), :], buffer.at[k], sems.at[k]) for k in range(2)
    ]
    copies.append(pltpu.make_async_copy(prev.at[0], rows, sems.at[2]))
    copies.append(pltpu.make_async_copy(slots, ids, sems.at[3]))
    for copy in copies:
        copy.start()
    wanted = 2 * row + piece // 4
    columns = select_columns(col % 2)
    for copy in copies:
        copy.wait()
    rolled = pltpu.roll(rows[...], (16 - 2 * piece) % 16, 0)
    zero = jnp.zeros((32, 512), jnp.float32)
    chunk = jnp.where(ids[0, 2 * row] == wanted, buffer[0], zero)
    chunk = jnp.where(ids[0, 2 * row + 1] == wanted, buffer[1], chunk)
    out[...] = dot(jnp.concatenate([chunk, rolled[:8]], 0), columns)


def own_piece(slot_blocks, panel_blocks, prev_panel):
    return pl.pallas_call(
        piece_kernel,
        out_shape=jax.ShapeDtypeStruct((40, 256), jnp.float32),
        in_specs=[pl.BlockSpec(memory_space=pltpu.HBM)] * 3,
        out_specs=pl.BlockSpec(memory_space=pltpu.VMEM),
        scratch_shapes=[
            pltpu.SMEM((1, 64), jnp.int32),
            pltpu.VMEM((2, 32, 512), jnp.float32),
            pltpu.VMEM((16, 512), jnp.float32),
            pltpu.SemaphoreType.DMA((4,)),
        ],
        name="own_piece",
    )(slot_blocks, panel_blocks, prev_panel)


def factor_halves(slots, panel, row):
    first, second = panel[0, :BLK, :], panel[0, BLK:, :]
    zero = jnp.zeros_like(first)
    low = jnp.where(slots[0, 2 * row] == 2 * row, first, zero)
    high = jnp.where(slots[0, 2 * row + 1] == 2 * row + 1, second, zero)
    return low, jnp.where(slots[0, 2 * row] == 2 * row + 1, first, high)


def cross_kernel(slots, panel, top_column, top_diag, prev, out, mine, others):
    row = lax.axis_index("prow")
    core = lax.axis_index("pcol") % 2
    low, high = factor_halves(slots, panel, row)
    diag = pltpu.roll(top_diag[...], (512 - 16 * row) % 512, 1)[:, :16]
    part = dot(top_column[:, :BLK], low) + dot(top_column[:, BLK:], high) + dot(diag, prev[0])
    out[...] = part
    mine[...] = dot(part, select_columns(core))
    others[...] = dot(part, select_columns(1 - core))


def cross_rows(slot_blocks, panel_blocks, top_column, top_diag, prev_panel):
    return pl.pallas_call(
        cross_kernel,
        out_shape=(
            jax.ShapeDtypeStruct((32, 512), jnp.float32),
            jax.ShapeDtypeStruct((32, 256), jnp.float32),
            jax.ShapeDtypeStruct((32, 256), jnp.float32),
        ),
        in_specs=[pl.BlockSpec(memory_space=pltpu.SMEM)] + [pl.BlockSpec(memory_space=pltpu.VMEM)] * 4,
        out_specs=(pl.BlockSpec(memory_space=pltpu.VMEM),) * 3,
        compiler_params=kernel_params,
        name="cross_rows",
    )(slot_blocks, panel_blocks, top_column, top_diag, prev_panel)


def gather_kernel(spread, cross_own, cross_other, cross_part, prev, out):
    core = lax.axis_index("pcol") % 2
    for k in range(ROWS):
        out[k, :40, :] = spread[:, 128 * (k % 2) : 128 * (k % 2) + 128]
        out[k, 40:, :] = jnp.zeros((8, 128), jnp.float32)
    mine, others = cross_own[...], cross_other[...]
    pair = [jnp.where(core == 0, mine, others), jnp.where(core == 0, others, mine)]
    part = cross_part[...]
    for k in range(ROWS):
        for lane in range(2):
            for who in range(2):
                at = 34 + 2 * who + lane
                out[k, at : at + 1, :] = pair[who][k : k + 1, 128 * lane : 128 * lane + 128]
        for lane in range(4):
            span = slice(128 * lane, 128 * lane + 128)
            out[k, 38 + lane : 39 + lane, :] = prev[0, k % 16 : k % 16 + 1, span]
            out[k, 42 + lane : 43 + lane, :] = part[k : k + 1, span]


def gather_operand(spread, cross_own, cross_other, cross_part, prev_panel):
    return pl.pallas_call(
        gather_kernel,
        out_shape=jax.ShapeDtypeStruct((ROWS, 48, 128), jnp.float32),
        in_specs=[pl.BlockSpec(memory_space=pltpu.VMEM)] * 5,
        out_specs=pl.BlockSpec(memory_space=pltpu.VMEM),
        compiler_params=kernel_params,
        name="gather_operand",
    )(spread, cross_own, cross_other, cross_part, prev_panel)


def product_kernel(got, mine, mine_b, next_z, next_zb, out, cross_full, stride, prev_rows):
    row = lax.axis_index("prow")
    core = lax.axis_index("pcol") % 2
    half = row % 2
    for k in range(ROWS):
        prev_rows[2 * k : 2 * k + 2, :] = got[k, 32:34, :]
    own = got[pl.ds(16 * core, 16), :32, :].reshape(512, 128)
    other = got[pl.ds(16 - 16 * core, 16), :32, :].reshape(512, 128)
    own_prev = prev_rows[pl.ds(pl.multiple_of(32 * core, 32), 32), :]
    other_prev = prev_rows[pl.ds(pl.multiple_of(32 - 32 * core, 32), 32), :]
    prev = jnp.concatenate([own_prev, other_prev], 0)
    sums = -jnp.sum(got[:, 32:48, :], 0)
    cross = jnp.concatenate([sums[2:6], jnp.zeros((4, 128), jnp.float32)], 0)
    cross_full[...] = sums[10:14]
    for c in range(COLS):
        stride[4 * c : 4 * c + 4, :] = got[2 * c + row // 16, 38:42, :]
    for left, right, which in ((mine, mine_b, half), (next_z, next_zb, 1 - half)):
        top = jnp.concatenate([left[256:, :256], left[256:, 256:], right[256:, :256], right[256:, 256:]], 0)
        part = dot(left[:256, :], own) + dot(right[:256, :], other) + dot(top.T, prev)
        part = part.T
        for y in range(YS):
            out[2 * y + which, :16, :] = part[16 * y : 16 * y + 16, :128]
            out[2 * y + which, 16:32, :] = part[16 * y : 16 * y + 16, 128:]
            out[2 * y + which, 32:, :] = cross


def column_product(got, mine, mine_b, next_z, next_zb):
    return pl.pallas_call(
        product_kernel,
        out_shape=(
            jax.ShapeDtypeStruct((16, 40, 128), jnp.float32),
            jax.ShapeDtypeStruct((4, 128), jnp.float32),
            jax.ShapeDtypeStruct((64, 128), jnp.float32),
        ),
        in_specs=[pl.BlockSpec(memory_space=pltpu.VMEM)] * 5,
        out_specs=(pl.BlockSpec(memory_space=pltpu.VMEM),) * 3,
        scratch_shapes=[pltpu.VMEM((64, 128), jnp.float32)],
        compiler_params=kernel_params,
        name="column_product",
    )(got, mine, mine_b, next_z, next_zb)


def diag_kernel(slots, panel, got, cross_full, stride, fresh_out, out, columns):
    row = lax.axis_index("prow")
    half = row % 2
    y = lax.axis_index("pcol") // 2
    fresh = []
    for h in range(2):
        total = got[h, :32, :]
        for k in range(1, YS):
            total = total + got[2 * k + h, :32, :]
        fresh.append(jnp.concatenate([-total[:16], -total[16:]], 1))
    fresh = jnp.concatenate(fresh, 0)
    fresh_out[0] = fresh
    low, high = factor_halves(slots, panel, row)
    part = dot(fresh[:, :BLK], low) + dot(fresh[:, BLK:], high)
    for k in range(YS):
        block = got[2 * k + half, 32:40, :]
        for who in range(2):
            for h in range(2):
                columns[h, 2 * k + who : 2 * k + who + 1, :] = block[2 * who + h : 2 * who + h + 1]
    rows = jnp.concatenate([stride[pl.ds(lane, 16, stride=4), :] for lane in range(4)], 1)
    own = []
    for h in range(2):
        columns[2 + h, :, :] = jnp.zeros((128, 128), jnp.float32)
        columns[2 + h, :, :16] = columns[h, :16, :].T
        picked = columns[2 + h, pl.ds(pl.multiple_of(16 * y, 16), 16), :]
        own.append(dot(picked[:, :16], rows))
    part = part + jnp.concatenate(own, 0)
    for k in range(ROWS):
        for lane in range(4):
            out[k, lane : lane + 1, :] = part[k : k + 1, 128 * lane : 128 * lane + 128]
        out[k, 4:8, :] = cross_full[...]


def diag_operand(slot_blocks, panel_blocks, got, cross_full, stride):
    return pl.pallas_call(
        diag_kernel,
        out_shape=(
            jax.ShapeDtypeStruct((1, 32, 256), jnp.float32),
            jax.ShapeDtypeStruct((ROWS, 8, 128), jnp.float32),
        ),
        in_specs=[pl.BlockSpec(memory_space=pltpu.SMEM)] + [pl.BlockSpec(memory_space=pltpu.VMEM)] * 4,
        out_specs=(pl.BlockSpec(memory_space=pltpu.VMEM),) * 2,
        scratch_shapes=[pltpu.VMEM((4, 128, 128), jnp.float32)],
        compiler_params=kernel_params,
        name="diag_operand",
    )(slot_blocks, panel_blocks, got, cross_full, stride)


def step(pool_inverse, panel_blocks, prev_panel, pivot_inverse, top_column, top_diag, slot_blocks):
    core_swap = [(i, i ^ 1) for i in range(COLS)]
    row_swap = [(i, i ^ 1) for i in range(ROWS)]

    sent = own_piece(slot_blocks, panel_blocks, prev_panel)
    sent, top_column, top_diag = lax.optimization_barrier((sent, top_column, top_diag))
    spread = lax.ppermute(sent, ("prow", "pcol"), spread_pairs())

    blocks = jnp.concatenate([pool_inverse, jnp.concatenate([top_column[:16], top_column[16:]], 1)], 0)
    blocks_z = lax.ppermute(blocks, "prow", row_swap)
    blocks_b = lax.ppermute(blocks, "pcol", core_swap)

    cross_part, cross_own, cross_sent = cross_rows(slot_blocks, panel_blocks, top_column, top_diag, prev_panel)
    cross_other = lax.ppermute(cross_sent, "pcol", core_swap)

    send = gather_operand(spread, cross_own, cross_other, cross_part, prev_panel)
    got = lax.all_to_all(send, "prow", 0, 0, tiled=True)
    blocks_zb = lax.ppermute(blocks_z, "pcol", core_swap)

    send, cross_full, stride = column_product(got, blocks, blocks_b, blocks_z, blocks_zb)
    groups = [
        [(x * 8 + 2 * z + h) * COLS + 2 * i + k for i in range(YS) for h in range(2)]
        for x in range(4)
        for z in range(4)
        for k in range(2)
    ]
    got = lax.all_to_all(send, ("prow", "pcol"), 0, 0, tiled=True, axis_index_groups=groups)
    fresh, send = diag_operand(slot_blocks, panel_blocks, got, cross_full, stride)
    got = lax.all_to_all(send, "prow", 0, 0, tiled=True)
    cross_out = got[:, 4:].reshape(1, 32, 512)
    total = jnp.sum(got[:, :4], 0)
    got = lax.all_to_all(jnp.broadcast_to(total, (ROWS, 4, 128)), "prow", 0, 0, tiled=True)
    diag_out = pivot_inverse - got.reshape(1, 32, 512)
    return fresh, cross_out, diag_out


def solution(mesh):
    in_specs = (
        P("prow", "pcol"),
        P(None, "prow", None),
        P(None, "prow", None),
        P(None, "pcol", None),
        P("pcol", "prow"),
        P("pcol", None),
        P(),
    )
    out_specs = (P(None, "pcol", "prow"), P(None, "pcol", None), P(None, "pcol", None))
    return jax.shard_map(step, mesh=mesh, in_specs=in_specs, out_specs=out_specs, check_vma=False)
```

```python
import jax
import jax.numpy as jnp
from jax import lax
from jax.experimental import pallas as pl
from jax.experimental.pallas import tpu as pltpu
from jax.sharding import PartitionSpec as P


BLK = 128
ROWS = 32
COLS = 16
YS = 8

highest = lax.Precision.HIGHEST
kernel_params = pltpu.CompilerParams(vmem_limit_bytes=16 << 20)


def spread_pairs():
    pairs = []
    for row in range(ROWS):
        for col in range(COLS):
            y, q, z = row // 4, row % 4, row % 8
            t = (col // 2 - y - 4 + z) % 8
            pairs.append((row * COLS + col, (8 * q + t) * COLS + 2 * y + col % 2))
    return pairs


def select_columns(core):
    source = lax.broadcasted_iota(jnp.int32, (512, 256), 0)
    n = lax.broadcasted_iota(jnp.int32, (512, 256), 1)
    wanted = 64 * ((n % 128) // 16) + 32 * core + 16 * (n // 128) + n % 16
    return (source == wanted).astype(jnp.float32)


def dot(left, right):
    return jnp.dot(left, right, precision=highest, preferred_element_type=jnp.float32)


def piece_kernel(slots, panel, prev, out, ids, buffer, rows, sems):
    row = lax.axis_index("prow")
    col = lax.axis_index("pcol")
    piece = (col // 2 + 16 - row // 4 - 4 + row % 8) % 8
    offset = 32 * (piece % 4)
    copies = [
        pltpu.make_async_copy(panel.at[0, pl.ds(BLK * k + offset, 32), :], buffer.at[k], sems.at[k]) for k in range(2)
    ]
    copies.append(pltpu.make_async_copy(prev.at[0], rows, sems.at[2]))
    copies.append(pltpu.make_async_copy(slots, ids, sems.at[3]))
    for copy in copies:
        copy.start()
    wanted = 2 * row + piece // 4
    columns = select_columns(col % 2)
    for copy in copies:
        copy.wait()
    rolled = pltpu.roll(rows[...], (16 - 4 * (piece // 2)) % 16, 0)
    zero = jnp.zeros((32, 512), jnp.float32)
    chunk = jnp.where(ids[0, 2 * row] == wanted, buffer[0], zero)
    chunk = jnp.where(ids[0, 2 * row + 1] == wanted, buffer[1], chunk)
    out[...] = dot(jnp.concatenate([chunk, rolled[:8]], 0), columns)


def own_piece(slot_blocks, panel_blocks, prev_panel):
    return pl.pallas_call(
        piece_kernel,
        out_shape=jax.ShapeDtypeStruct((40, 256), jnp.float32),
        in_specs=[pl.BlockSpec(memory_space=pltpu.HBM)] * 3,
        out_specs=pl.BlockSpec(memory_space=pltpu.VMEM),
        scratch_shapes=[
            pltpu.SMEM((1, 64), jnp.int32),
            pltpu.VMEM((2, 32, 512), jnp.float32),
            pltpu.VMEM((16, 512), jnp.float32),
            pltpu.SemaphoreType.DMA((4,)),
        ],
        name="own_piece",
    )(slot_blocks, panel_blocks, prev_panel)


def factor_halves(slots, panel, row):
    first, second = panel[0, :BLK, :], panel[0, BLK:, :]
    zero = jnp.zeros_like(first)
    low = jnp.where(slots[0, 2 * row] == 2 * row, first, zero)
    high = jnp.where(slots[0, 2 * row + 1] == 2 * row + 1, second, zero)
    return low, jnp.where(slots[0, 2 * row] == 2 * row + 1, first, high)


def cross_kernel(slots, panel, top_column, top_diag, prev, mine, others):
    row = lax.axis_index("prow")
    core = lax.axis_index("pcol") % 2
    low, high = factor_halves(slots, panel, row)
    diag = pltpu.roll(top_diag[...], (512 - 16 * row) % 512, 1)[:, :16]
    part = dot(top_column[:, :BLK], low) + dot(top_column[:, BLK:], high) + dot(diag, prev[0])
    mine[...] = dot(part, select_columns(core))
    others[...] = dot(part, select_columns(1 - core))


def cross_rows(slot_blocks, panel_blocks, top_column, top_diag, prev_panel):
    return pl.pallas_call(
        cross_kernel,
        out_shape=(
            jax.ShapeDtypeStruct((32, 256), jnp.float32),
            jax.ShapeDtypeStruct((32, 256), jnp.float32),
        ),
        in_specs=[pl.BlockSpec(memory_space=pltpu.SMEM)] + [pl.BlockSpec(memory_space=pltpu.VMEM)] * 4,
        out_specs=(pl.BlockSpec(memory_space=pltpu.VMEM),) * 2,
        compiler_params=kernel_params,
        name="cross_rows",
    )(slot_blocks, panel_blocks, top_column, top_diag, prev_panel)


def gather_kernel(spread, cross_own, cross_other, prev, out):
    row = lax.axis_index("prow")
    core = lax.axis_index("pcol") % 2
    mine, others = cross_own[...], cross_other[...]
    pair = [jnp.where(core == 0, mine, others), jnp.where(core == 0, others, mine)]
    for k in range(ROWS):
        out[k, :36, :] = spread[:36, 128 * (k % 2) : 128 * (k % 2) + 128]
        for lane in range(2):
            for who in range(2):
                at = 36 + 2 * who + lane
                out[k, at : at + 1, :] = pair[who][k : k + 1, 128 * lane : 128 * lane + 128]
    for parity in range(2):

        @pl.when(row % 2 == parity)
        def _():
            for k in range(16):
                for lane in range(4):
                    span = slice(128 * lane, 128 * lane + 128)
                    out[16 * parity + k, 32 + lane : 33 + lane, :] = prev[0, k : k + 1, span]


def gather_operand(spread, cross_own, cross_other, prev_panel):
    return pl.pallas_call(
        gather_kernel,
        out_shape=jax.ShapeDtypeStruct((ROWS, 40, 128), jnp.float32),
        in_specs=[pl.BlockSpec(memory_space=pltpu.VMEM)] * 4,
        out_specs=pl.BlockSpec(memory_space=pltpu.VMEM),
        compiler_params=kernel_params,
        name="gather_operand",
    )(spread, cross_own, cross_other, prev_panel)


def product_kernel(got, mine, mine_b, next_z, next_zb, out, cross_keep, cross_give, stride, prev_rows):
    row = lax.axis_index("prow")
    core = lax.axis_index("pcol") % 2
    half = row % 2
    strided = row // 16
    for k in range(COLS):
        stride[4 * k : 4 * k + 4, :] = got[2 * k + strided, 32:36, :]
        prev_rows[4 * k : 4 * k + 4, :] = got[2 * k + 1 - strided, 32:36, :]
    own = got[pl.ds(16 * core, 16), :32, :].reshape(512, 128)
    other = got[pl.ds(16 - 16 * core, 16), :32, :].reshape(512, 128)
    own_prev = prev_rows[pl.ds(pl.multiple_of(32 * core, 32), 32), :]
    other_prev = prev_rows[pl.ds(pl.multiple_of(32 - 32 * core, 32), 32), :]
    prev = jnp.concatenate([own_prev, other_prev], 0)
    sums = -jnp.sum(got[:, 32:40, :], 0)
    pad = jnp.zeros((4, 128), jnp.float32)
    cross = jnp.concatenate([sums[4:8], pad], 0)
    swapped = jnp.concatenate([sums[6:8], sums[4:6], pad], 0)
    cross_keep[...] = jnp.where(core == 0, cross, swapped)
    cross_give[...] = jnp.where(core == 0, swapped, cross)
    for left, right, which in ((mine, mine_b, half), (next_z, next_zb, 1 - half)):
        top = jnp.concatenate([left[256:, :256], left[256:, 256:], right[256:, :256], right[256:, 256:]], 0)
        part = dot(left[:256, :], own) + dot(right[:256, :], other) + dot(top.T, prev)
        part = part.T
        for y in range(YS):
            out[2 * y + which, :16, :] = part[16 * y : 16 * y + 16, :128]
            out[2 * y + which, 16:32, :] = part[16 * y : 16 * y + 16, 128:]
            out[2 * y + which, 32:, :] = cross


def column_product(got, mine, mine_b, next_z, next_zb):
    return pl.pallas_call(
        product_kernel,
        out_shape=(
            jax.ShapeDtypeStruct((16, 40, 128), jnp.float32),
            jax.ShapeDtypeStruct((8, 128), jnp.float32),
            jax.ShapeDtypeStruct((8, 128), jnp.float32),
            jax.ShapeDtypeStruct((64, 128), jnp.float32),
        ),
        in_specs=[pl.BlockSpec(memory_space=pltpu.VMEM)] * 5,
        out_specs=(pl.BlockSpec(memory_space=pltpu.VMEM),) * 4,
        scratch_shapes=[pltpu.VMEM((64, 128), jnp.float32)],
        compiler_params=kernel_params,
        name="column_product",
    )(got, mine, mine_b, next_z, next_zb)


def diag_kernel(slots, panel, got, cross_keep, cross_got, stride, fresh_out, out, columns):
    row = lax.axis_index("prow")
    half = row % 2
    y = lax.axis_index("pcol") // 2
    core = lax.axis_index("pcol") % 2
    fresh = []
    for h in range(2):
        total = got[h, :32, :]
        for k in range(1, YS):
            total = total + got[2 * k + h, :32, :]
        fresh.append(jnp.concatenate([-total[:16], -total[16:]], 1))
    fresh = jnp.concatenate(fresh, 0)
    fresh_out[0] = fresh
    low, high = factor_halves(slots, panel, row)
    part = dot(fresh[:, :BLK], low) + dot(fresh[:, BLK:], high)
    for k in range(YS):
        block = got[2 * k + half, 32:40, :]
        for who in range(2):
            for h in range(2):
                columns[h, 2 * k + who : 2 * k + who + 1, :] = block[2 * who + h : 2 * who + h + 1]
    rows = jnp.concatenate([stride[pl.ds(lane, 16, stride=4), :] for lane in range(4)], 1)
    own = []
    for h in range(2):
        columns[2 + h, :, :] = jnp.zeros((128, 128), jnp.float32)
        columns[2 + h, :, :16] = columns[h, :16, :].T
        picked = columns[2 + h, pl.ds(pl.multiple_of(16 * y, 16), 16), :]
        own.append(dot(picked[:, :16], rows))
    part = part + jnp.concatenate(own, 0)
    lane = lax.broadcasted_iota(jnp.int32, (128, 512), 0)
    spot = (lax.broadcasted_iota(jnp.int32, (128, 512), 1) == 64 * (lane // 16) + lane % 16).astype(jnp.float32)
    placed = dot(jnp.concatenate([cross_keep[:2, :], cross_got[:2, :], jnp.zeros((4, 128), jnp.float32)], 0), spot)
    ours = placed[0:1] + pltpu.roll(placed[1:2], 16, 1)
    theirs = placed[2:3] + pltpu.roll(placed[3:4], 16, 1)
    line = jnp.where(core == 0, ours + pltpu.roll(theirs, 32, 1), theirs + pltpu.roll(ours, 32, 1))
    line = jnp.concatenate([line[:, 128 * k : 128 * k + 128] for k in range(4)], 0)
    for k in range(ROWS):
        for lane in range(4):
            out[k, lane : lane + 1, :] = part[k : k + 1, 128 * lane : 128 * lane + 128]
        out[k, 4:8, :] = line


def diag_operand(slot_blocks, panel_blocks, got, cross_keep, cross_got, stride):
    return pl.pallas_call(
        diag_kernel,
        out_shape=(
            jax.ShapeDtypeStruct((1, 32, 256), jnp.float32),
            jax.ShapeDtypeStruct((ROWS, 8, 128), jnp.float32),
        ),
        in_specs=[pl.BlockSpec(memory_space=pltpu.SMEM)] + [pl.BlockSpec(memory_space=pltpu.VMEM)] * 5,
        out_specs=(pl.BlockSpec(memory_space=pltpu.VMEM),) * 2,
        scratch_shapes=[pltpu.VMEM((4, 128, 128), jnp.float32)],
        compiler_params=kernel_params,
        name="diag_operand",
    )(slot_blocks, panel_blocks, got, cross_keep, cross_got, stride)


def total_kernel(got, out, cross_out):
    total = jnp.sum(got[:, :4, :], 0)
    for k in range(ROWS):
        out[k] = total
        for lane in range(4):
            cross_out[0, k : k + 1, 128 * lane : 128 * lane + 128] = got[k, 4 + lane : 5 + lane, :]


def total_operand(got):
    return pl.pallas_call(
        total_kernel,
        out_shape=(
            jax.ShapeDtypeStruct((ROWS, 4, 128), jnp.float32),
            jax.ShapeDtypeStruct((1, 32, 512), jnp.float32),
        ),
        in_specs=[pl.BlockSpec(memory_space=pltpu.VMEM)],
        out_specs=(pl.BlockSpec(memory_space=pltpu.VMEM),) * 2,
        compiler_params=kernel_params,
        name="total_operand",
    )(got)


def last_kernel(got, pivot, out):
    for k in range(ROWS):
        for lane in range(4):
            span = slice(128 * lane, 128 * lane + 128)
            out[0, k : k + 1, span] = pivot[0, k : k + 1, span] - got[k, lane : lane + 1, :]


def last_step(got, pivot_inverse):
    return pl.pallas_call(
        last_kernel,
        out_shape=jax.ShapeDtypeStruct((1, 32, 512), jnp.float32),
        in_specs=[pl.BlockSpec(memory_space=pltpu.VMEM)] * 2,
        out_specs=pl.BlockSpec(memory_space=pltpu.VMEM),
        compiler_params=kernel_params,
        name="last_step",
    )(got, pivot_inverse)


def step(pool_inverse, panel_blocks, prev_panel, pivot_inverse, top_column, top_diag, slot_blocks):
    core_swap = [(i, i ^ 1) for i in range(COLS)]
    row_swap = [(i, i ^ 1) for i in range(ROWS)]

    sent = own_piece(slot_blocks, panel_blocks, prev_panel)
    sent, top_column, top_diag = lax.optimization_barrier((sent, top_column, top_diag))
    spread = lax.ppermute(sent, ("prow", "pcol"), spread_pairs())

    blocks = jnp.concatenate([pool_inverse, jnp.concatenate([top_column[:16], top_column[16:]], 1)], 0)
    blocks_z = lax.ppermute(blocks, "prow", row_swap)
    blocks_b = lax.ppermute(blocks, "pcol", core_swap)

    cross_own, cross_sent = cross_rows(slot_blocks, panel_blocks, top_column, top_diag, prev_panel)
    cross_other = lax.ppermute(cross_sent, "pcol", core_swap)

    send = gather_operand(spread, cross_own, cross_other, prev_panel)
    got = lax.all_to_all(send, "prow", 0, 0, tiled=True)
    blocks_zb = lax.ppermute(blocks_z, "pcol", core_swap)

    send, cross_keep, cross_give, stride = column_product(got, blocks, blocks_b, blocks_z, blocks_zb)
    groups = [
        [(x * 8 + 2 * z + h) * COLS + 2 * i + k for i in range(YS) for h in range(2)]
        for x in range(4)
        for z in range(4)
        for k in range(2)
    ]
    got = lax.all_to_all(send, ("prow", "pcol"), 0, 0, tiled=True, axis_index_groups=groups)
    cross_got = lax.ppermute(cross_give, "pcol", core_swap)
    fresh, send = diag_operand(slot_blocks, panel_blocks, got, cross_keep, cross_got, stride)
    got = lax.all_to_all(send, "prow", 0, 0, tiled=True)
    total, cross_out = total_operand(got)
    got = lax.all_to_all(total, "prow", 0, 0, tiled=True)
    return fresh, cross_out, last_step(got, pivot_inverse)


def solution(mesh):
    in_specs = (
        P("prow", "pcol"),
        P(None, "prow", None),
        P(None, "prow", None),
        P(None, "pcol", None),
        P("pcol", "prow"),
        P("pcol", None),
        P(),
    )
    out_specs = (P(None, "pcol", "prow"), P(None, "pcol", None), P(None, "pcol", None))
    return jax.shard_map(step, mesh=mesh, in_specs=in_specs, out_specs=out_specs, check_vma=False)
```

```python
import jax
import jax.numpy as jnp
from jax import lax
from jax.experimental import pallas as pl
from jax.experimental.pallas import tpu as pltpu
from jax.sharding import PartitionSpec as P


BLK = 128
ROWS = 32
COLS = 16
YS = 8

highest = lax.Precision.HIGHEST
kernel_params = pltpu.CompilerParams(vmem_limit_bytes=16 << 20)


def spread_pairs():
    pairs = []
    for row in range(ROWS):
        for col in range(COLS):
            y, q, z = row // 4, row % 4, row % 8
            t = (col // 2 - y - 4 + z) % 8
            pairs.append((row * COLS + col, (8 * q + t) * COLS + 2 * y + col % 2))
    return pairs


def select_columns(core):
    source = lax.broadcasted_iota(jnp.int32, (512, 256), 0)
    n = lax.broadcasted_iota(jnp.int32, (512, 256), 1)
    wanted = 64 * ((n % 128) // 16) + 32 * core + 16 * (n // 128) + n % 16
    return (source == wanted).astype(jnp.float32)


def dot(left, right):
    return jnp.dot(left, right, precision=highest, preferred_element_type=jnp.float32)


def piece_kernel(slots, panel, prev, out, ids, buffer, rows, sems):
    row = lax.axis_index("prow")
    col = lax.axis_index("pcol")
    piece = (col // 2 + 16 - row // 4 - 4 + row % 8) % 8
    offset = 32 * (piece % 4)
    copies = [
        pltpu.make_async_copy(panel.at[0, pl.ds(BLK * k + offset, 32), :], buffer.at[k], sems.at[k]) for k in range(2)
    ]
    copies.append(pltpu.make_async_copy(prev.at[0], rows, sems.at[2]))
    copies.append(pltpu.make_async_copy(slots, ids, sems.at[3]))
    for copy in copies:
        copy.start()
    wanted = 2 * row + piece // 4
    columns = select_columns(col % 2)
    for copy in copies:
        copy.wait()
    rolled = pltpu.roll(rows[...], (16 - 4 * (piece // 2)) % 16, 0)
    zero = jnp.zeros((32, 512), jnp.float32)
    chunk = jnp.where(ids[0, 2 * row] == wanted, buffer[0], zero)
    chunk = jnp.where(ids[0, 2 * row + 1] == wanted, buffer[1], chunk)
    out[...] = dot(jnp.concatenate([chunk, rolled[:8]], 0), columns)


def own_piece(slot_blocks, panel_blocks, prev_panel):
    return pl.pallas_call(
        piece_kernel,
        out_shape=jax.ShapeDtypeStruct((40, 256), jnp.float32),
        in_specs=[pl.BlockSpec(memory_space=pltpu.HBM)] * 3,
        out_specs=pl.BlockSpec(memory_space=pltpu.VMEM),
        scratch_shapes=[
            pltpu.SMEM((1, 64), jnp.int32),
            pltpu.VMEM((2, 32, 512), jnp.float32),
            pltpu.VMEM((16, 512), jnp.float32),
            pltpu.SemaphoreType.DMA((4,)),
        ],
        name="own_piece",
    )(slot_blocks, panel_blocks, prev_panel)


def factor_halves(slots, panel, row):
    first, second = panel[0, :BLK, :], panel[0, BLK:, :]
    zero = jnp.zeros_like(first)
    low = jnp.where(slots[0, 2 * row] == 2 * row, first, zero)
    high = jnp.where(slots[0, 2 * row + 1] == 2 * row + 1, second, zero)
    return low, jnp.where(slots[0, 2 * row] == 2 * row + 1, first, high)


def cross_kernel(slots, panel, top_column, top_diag, prev, mine, others):
    row = lax.axis_index("prow")
    core = lax.axis_index("pcol") % 2
    low, high = factor_halves(slots, panel, row)
    diag = pltpu.roll(top_diag[...], (512 - 16 * row) % 512, 1)[:, :16]
    part = dot(top_column[:, :BLK], low) + dot(top_column[:, BLK:], high) + dot(diag, prev[0])
    mine[...] = dot(part, select_columns(core))
    others[...] = dot(part, select_columns(1 - core))


def cross_rows(slot_blocks, panel_blocks, top_column, top_diag, prev_panel):
    return pl.pallas_call(
        cross_kernel,
        out_shape=(
            jax.ShapeDtypeStruct((32, 256), jnp.float32),
            jax.ShapeDtypeStruct((32, 256), jnp.float32),
        ),
        in_specs=[pl.BlockSpec(memory_space=pltpu.SMEM)] + [pl.BlockSpec(memory_space=pltpu.VMEM)] * 4,
        out_specs=(pl.BlockSpec(memory_space=pltpu.VMEM),) * 2,
        compiler_params=kernel_params,
        name="cross_rows",
    )(slot_blocks, panel_blocks, top_column, top_diag, prev_panel)


def gather_kernel(spread, cross_own, cross_other, prev, out):
    row = lax.axis_index("prow")
    core = lax.axis_index("pcol") % 2
    mine, others = cross_own[...], cross_other[...]
    pair = [jnp.where(core == 0, mine, others), jnp.where(core == 0, others, mine)]
    for k in range(ROWS):
        out[k, :36, :] = spread[:36, 128 * (k % 2) : 128 * (k % 2) + 128]
        for lane in range(2):
            for who in range(2):
                at = 36 + 2 * who + lane
                out[k, at : at + 1, :] = pair[who][k : k + 1, 128 * lane : 128 * lane + 128]
    for parity in range(2):

        @pl.when(row % 2 == parity)
        def _():
            for k in range(16):
                for lane in range(4):
                    span = slice(128 * lane, 128 * lane + 128)
                    out[16 * parity + k, 32 + lane : 33 + lane, :] = prev[0, k : k + 1, span]


def gather_operand(spread, cross_own, cross_other, prev_panel):
    return pl.pallas_call(
        gather_kernel,
        out_shape=jax.ShapeDtypeStruct((ROWS, 40, 128), jnp.float32),
        in_specs=[pl.BlockSpec(memory_space=pltpu.VMEM)] * 4,
        out_specs=pl.BlockSpec(memory_space=pltpu.VMEM),
        compiler_params=kernel_params,
        name="gather_operand",
    )(spread, cross_own, cross_other, prev_panel)


def product_kernel(got, mine, mine_b, next_z, next_zb, out, cross_pair, stride, prev_rows):
    row = lax.axis_index("prow")
    core = lax.axis_index("pcol") % 2
    half = row % 2
    strided = row // 16
    for k in range(COLS):
        stride[4 * k : 4 * k + 4, :] = got[2 * k + strided, 32:36, :]
        prev_rows[4 * k : 4 * k + 4, :] = got[2 * k + 1 - strided, 32:36, :]
    own = got[pl.ds(16 * core, 16), :32, :].reshape(512, 128)
    other = got[pl.ds(16 - 16 * core, 16), :32, :].reshape(512, 128)
    own_prev = prev_rows[pl.ds(pl.multiple_of(32 * core, 32), 32), :]
    other_prev = prev_rows[pl.ds(pl.multiple_of(32 - 32 * core, 32), 32), :]
    prev = jnp.concatenate([own_prev, other_prev], 0)
    sums = -jnp.sum(got[:, 32:40, :], 0)
    pad = jnp.zeros((4, 128), jnp.float32)
    cross = jnp.concatenate([sums[4:8], pad], 0)
    cross_pair[...] = cross
    for left, right, which in ((mine, mine_b, half), (next_z, next_zb, 1 - half)):
        top = jnp.concatenate([left[256:, :256], left[256:, 256:], right[256:, :256], right[256:, 256:]], 0)
        part = dot(left[:256, :], own) + dot(right[:256, :], other) + dot(top.T, prev)
        part = part.T
        for y in range(YS):
            out[2 * y + which, :16, :] = part[16 * y : 16 * y + 16, :128]
            out[2 * y + which, 16:32, :] = part[16 * y : 16 * y + 16, 128:]
            out[2 * y + which, 32:, :] = cross


def column_product(got, mine, mine_b, next_z, next_zb):
    return pl.pallas_call(
        product_kernel,
        out_shape=(
            jax.ShapeDtypeStruct((16, 40, 128), jnp.float32),
            jax.ShapeDtypeStruct((8, 128), jnp.float32),
            jax.ShapeDtypeStruct((64, 128), jnp.float32),
        ),
        in_specs=[pl.BlockSpec(memory_space=pltpu.VMEM)] * 5,
        out_specs=(pl.BlockSpec(memory_space=pltpu.VMEM),) * 3,
        scratch_shapes=[pltpu.VMEM((64, 128), jnp.float32)],
        compiler_params=kernel_params,
        name="column_product",
    )(got, mine, mine_b, next_z, next_zb)


def diag_kernel(slots, panel, got, cross_pair, stride, fresh_out, out, columns):
    row = lax.axis_index("prow")
    half = row % 2
    y = lax.axis_index("pcol") // 2
    fresh = []
    for h in range(2):
        total = got[h, :32, :]
        for k in range(1, YS):
            total = total + got[2 * k + h, :32, :]
        fresh.append(jnp.concatenate([-total[:16], -total[16:]], 1))
    fresh = jnp.concatenate(fresh, 0)
    fresh_out[0] = fresh
    low, high = factor_halves(slots, panel, row)
    part = dot(fresh[:, :BLK], low) + dot(fresh[:, BLK:], high)
    for k in range(YS):
        block = got[2 * k + half, 32:40, :]
        for who in range(2):
            for h in range(2):
                columns[h, 2 * k + who : 2 * k + who + 1, :] = block[2 * who + h : 2 * who + h + 1]
    rows = jnp.concatenate([stride[pl.ds(lane, 16, stride=4), :] for lane in range(4)], 1)
    own = []
    for h in range(2):
        columns[2 + h, :, :] = jnp.zeros((128, 128), jnp.float32)
        columns[2 + h, :, :16] = columns[h, :16, :].T
        picked = columns[2 + h, pl.ds(pl.multiple_of(16 * y, 16), 16), :]
        own.append(dot(picked[:, :16], rows))
    part = part + jnp.concatenate(own, 0)
    for k in range(ROWS):
        for lane in range(4):
            out[k, lane : lane + 1, :] = part[k : k + 1, 128 * lane : 128 * lane + 128]
        out[k, 4:8, :] = cross_pair[:4, :]


def diag_operand(slot_blocks, panel_blocks, got, cross_pair, stride):
    return pl.pallas_call(
        diag_kernel,
        out_shape=(
            jax.ShapeDtypeStruct((1, 32, 256), jnp.float32),
            jax.ShapeDtypeStruct((ROWS, 8, 128), jnp.float32),
        ),
        in_specs=[pl.BlockSpec(memory_space=pltpu.SMEM)] + [pl.BlockSpec(memory_space=pltpu.VMEM)] * 4,
        out_specs=(pl.BlockSpec(memory_space=pltpu.VMEM),) * 2,
        scratch_shapes=[pltpu.VMEM((4, 128, 128), jnp.float32)],
        compiler_params=kernel_params,
        name="diag_operand",
    )(slot_blocks, panel_blocks, got, cross_pair, stride)


def total_kernel(got, out, keep, give):
    core = lax.axis_index("pcol") % 2
    total = jnp.sum(got[:, :4, :], 0)
    for k in range(ROWS):
        out[k] = total
        for lane in range(2):
            span = slice(128 * lane, 128 * lane + 128)
            first, second = got[k, 4 + lane : 5 + lane, :], got[k, 6 + lane : 7 + lane, :]
            keep[k : k + 1, span] = jnp.where(core == 0, first, second)
            give[k : k + 1, span] = jnp.where(core == 0, second, first)


def total_operand(got):
    return pl.pallas_call(
        total_kernel,
        out_shape=(
            jax.ShapeDtypeStruct((ROWS, 4, 128), jnp.float32),
            jax.ShapeDtypeStruct((32, 256), jnp.float32),
            jax.ShapeDtypeStruct((32, 256), jnp.float32),
        ),
        in_specs=[pl.BlockSpec(memory_space=pltpu.VMEM)],
        out_specs=(pl.BlockSpec(memory_space=pltpu.VMEM),) * 3,
        compiler_params=kernel_params,
        name="total_operand",
    )(got)


def place_columns(core):
    n = lax.broadcasted_iota(jnp.int32, (256, 512), 0)
    target = lax.broadcasted_iota(jnp.int32, (256, 512), 1)
    return (target == 64 * ((n % 128) // 16) + 32 * core + 16 * (n // 128) + n % 16).astype(jnp.float32)


def line_kernel(keep, taken, out):
    core = lax.axis_index("pcol") % 2
    out[0] = dot(keep[...], place_columns(core)) + dot(taken[...], place_columns(1 - core))


def cross_lines(keep, taken):
    return pl.pallas_call(
        line_kernel,
        out_shape=jax.ShapeDtypeStruct((1, 32, 512), jnp.float32),
        in_specs=[pl.BlockSpec(memory_space=pltpu.VMEM)] * 2,
        out_specs=pl.BlockSpec(memory_space=pltpu.VMEM),
        compiler_params=kernel_params,
        name="cross_lines",
    )(keep, taken)


def last_kernel(got, pivot, out):
    for k in range(ROWS):
        for lane in range(4):
            span = slice(128 * lane, 128 * lane + 128)
            out[0, k : k + 1, span] = pivot[0, k : k + 1, span] - got[k, lane : lane + 1, :]


def last_step(got, pivot_inverse):
    return pl.pallas_call(
        last_kernel,
        out_shape=jax.ShapeDtypeStruct((1, 32, 512), jnp.float32),
        in_specs=[pl.BlockSpec(memory_space=pltpu.VMEM)] * 2,
        out_specs=pl.BlockSpec(memory_space=pltpu.VMEM),
        compiler_params=kernel_params,
        name="last_step",
    )(got, pivot_inverse)


def step(pool_inverse, panel_blocks, prev_panel, pivot_inverse, top_column, top_diag, slot_blocks):
    core_swap = [(i, i ^ 1) for i in range(COLS)]
    row_swap = [(i, i ^ 1) for i in range(ROWS)]

    sent = own_piece(slot_blocks, panel_blocks, prev_panel)
    sent, top_column, top_diag = lax.optimization_barrier((sent, top_column, top_diag))
    spread = lax.ppermute(sent, ("prow", "pcol"), spread_pairs())

    blocks = jnp.concatenate([pool_inverse, jnp.concatenate([top_column[:16], top_column[16:]], 1)], 0)
    blocks_z = lax.ppermute(blocks, "prow", row_swap)
    blocks_b = lax.ppermute(blocks, "pcol", core_swap)

    cross_own, cross_sent = cross_rows(slot_blocks, panel_blocks, top_column, top_diag, prev_panel)
    cross_other = lax.ppermute(cross_sent, "pcol", core_swap)

    send = gather_operand(spread, cross_own, cross_other, prev_panel)
    got = lax.all_to_all(send, "prow", 0, 0, tiled=True)
    blocks_zb = lax.ppermute(blocks_z, "pcol", core_swap)

    send, cross_pair, stride = column_product(got, blocks, blocks_b, blocks_z, blocks_zb)
    groups = [
        [(x * 8 + 2 * z + h) * COLS + 2 * i + k for i in range(YS) for h in range(2)]
        for x in range(4)
        for z in range(4)
        for k in range(2)
    ]
    got = lax.all_to_all(send, ("prow", "pcol"), 0, 0, tiled=True, axis_index_groups=groups)
    fresh, send = diag_operand(slot_blocks, panel_blocks, got, cross_pair, stride)
    got = lax.all_to_all(send, "prow", 0, 0, tiled=True)
    total, keep, give = total_operand(got)
    got = lax.all_to_all(total, "prow", 0, 0, tiled=True)
    taken = lax.ppermute(give, "pcol", core_swap)
    cross_out = cross_lines(keep, taken)
    return fresh, cross_out, last_step(got, pivot_inverse)


def solution(mesh):
    in_specs = (
        P("prow", "pcol"),
        P(None, "prow", None),
        P(None, "prow", None),
        P(None, "pcol", None),
        P("pcol", "prow"),
        P("pcol", None),
        P(),
    )
    out_specs = (P(None, "pcol", "prow"), P(None, "pcol", None), P(None, "pcol", None))
    return jax.shard_map(step, mesh=mesh, in_specs=in_specs, out_specs=out_specs, check_vma=False)
```

```python
import jax
import jax.numpy as jnp
from jax import lax
from jax.experimental import pallas as pl
from jax.experimental.pallas import tpu as pltpu
from jax.sharding import PartitionSpec as P


BLK = 128
ROWS = 32
COLS = 16
YS = 8

highest = lax.Precision.HIGHEST
kernel_params = pltpu.CompilerParams(vmem_limit_bytes=16 << 20)


def spread_pairs():
    pairs = []
    for row in range(ROWS):
        for col in range(COLS):
            y, q, z = row // 4, row % 4, row % 8
            t = (col // 2 - y - 4 + z) % 8
            pairs.append((row * COLS + col, (8 * q + t) * COLS + 2 * y + col % 2))
    return pairs


def select_columns(core):
    source = lax.broadcasted_iota(jnp.int32, (512, 256), 0)
    n = lax.broadcasted_iota(jnp.int32, (512, 256), 1)
    wanted = 64 * ((n % 128) // 16) + 32 * core + 16 * (n // 128) + n % 16
    return (source == wanted).astype(jnp.float32)


def dot(left, right):
    return jnp.dot(left, right, precision=highest, preferred_element_type=jnp.float32)


def piece_kernel(slots, panel, prev, out, ids, buffer, rows, sems):
    row = lax.axis_index("prow")
    col = lax.axis_index("pcol")
    piece = (col // 2 + 16 - row // 4 - 4 + row % 8) % 8
    offset = 32 * (piece % 4)
    copies = [
        pltpu.make_async_copy(panel.at[0, pl.ds(BLK * k + offset, 32), :], buffer.at[k], sems.at[k]) for k in range(2)
    ]
    copies.append(pltpu.make_async_copy(prev.at[0], rows, sems.at[2]))
    copies.append(pltpu.make_async_copy(slots, ids, sems.at[3]))
    for copy in copies:
        copy.start()
    wanted = 2 * row + piece // 4
    columns = select_columns(col % 2)
    for copy in copies:
        copy.wait()
    rolled = pltpu.roll(rows[...], (16 - 4 * (piece // 2)) % 16, 0)
    zero = jnp.zeros((32, 512), jnp.float32)
    chunk = jnp.where(ids[0, 2 * row] == wanted, buffer[0], zero)
    chunk = jnp.where(ids[0, 2 * row + 1] == wanted, buffer[1], chunk)
    out[...] = dot(jnp.concatenate([chunk, rolled[:8]], 0), columns)


def own_piece(slot_blocks, panel_blocks, prev_panel):
    return pl.pallas_call(
        piece_kernel,
        out_shape=jax.ShapeDtypeStruct((40, 256), jnp.float32),
        in_specs=[pl.BlockSpec(memory_space=pltpu.HBM)] * 3,
        out_specs=pl.BlockSpec(memory_space=pltpu.VMEM),
        scratch_shapes=[
            pltpu.SMEM((1, 64), jnp.int32),
            pltpu.VMEM((2, 32, 512), jnp.float32),
            pltpu.VMEM((16, 512), jnp.float32),
            pltpu.SemaphoreType.DMA((4,)),
        ],
        name="own_piece",
    )(slot_blocks, panel_blocks, prev_panel)


def factor_halves(slots, panel, row):
    first, second = panel[0, :BLK, :], panel[0, BLK:, :]
    zero = jnp.zeros_like(first)
    low = jnp.where(slots[0, 2 * row] == 2 * row, first, zero)
    high = jnp.where(slots[0, 2 * row + 1] == 2 * row + 1, second, zero)
    return low, jnp.where(slots[0, 2 * row] == 2 * row + 1, first, high)


def cross_kernel(slots, panel, top_column, top_diag, prev, mine, others):
    row = lax.axis_index("prow")
    core = lax.axis_index("pcol") % 2
    low, high = factor_halves(slots, panel, row)
    diag = pltpu.roll(top_diag[...], (512 - 16 * row) % 512, 1)[:, :16]
    part = dot(top_column[:, :BLK], low) + dot(top_column[:, BLK:], high) + dot(diag, prev[0])
    shifted = jnp.where(core == 0, pltpu.roll(part, 480, 1), pltpu.roll(part, 32, 1))
    both = dot(jnp.concatenate([part, shifted], 0), select_columns(core))
    mine[...] = both[:32]
    others[...] = both[32:]


def cross_rows(slot_blocks, panel_blocks, top_column, top_diag, prev_panel):
    return pl.pallas_call(
        cross_kernel,
        out_shape=(
            jax.ShapeDtypeStruct((32, 256), jnp.float32),
            jax.ShapeDtypeStruct((32, 256), jnp.float32),
        ),
        in_specs=[pl.BlockSpec(memory_space=pltpu.SMEM)] + [pl.BlockSpec(memory_space=pltpu.VMEM)] * 4,
        out_specs=(pl.BlockSpec(memory_space=pltpu.VMEM),) * 2,
        compiler_params=kernel_params,
        name="cross_rows",
    )(slot_blocks, panel_blocks, top_column, top_diag, prev_panel)


def gather_kernel(spread, cross_own, cross_other, prev, out):
    row = lax.axis_index("prow")
    core = lax.axis_index("pcol") % 2
    mine, others = cross_own[...], cross_other[...]
    pair = [jnp.where(core == 0, mine, others), jnp.where(core == 0, others, mine)]
    for k in range(ROWS):
        out[k, :36, :] = spread[:36, 128 * (k % 2) : 128 * (k % 2) + 128]
        for lane in range(2):
            for who in range(2):
                at = 36 + 2 * who + lane
                out[k, at : at + 1, :] = pair[who][k : k + 1, 128 * lane : 128 * lane + 128]
    for parity in range(2):

        @pl.when(row % 2 == parity)
        def _():
            for k in range(16):
                for lane in range(4):
                    span = slice(128 * lane, 128 * lane + 128)
                    out[16 * parity + k, 32 + lane : 33 + lane, :] = prev[0, k : k + 1, span]


def gather_operand(spread, cross_own, cross_other, prev_panel):
    return pl.pallas_call(
        gather_kernel,
        out_shape=jax.ShapeDtypeStruct((ROWS, 40, 128), jnp.float32),
        in_specs=[pl.BlockSpec(memory_space=pltpu.VMEM)] * 4,
        out_specs=pl.BlockSpec(memory_space=pltpu.VMEM),
        compiler_params=kernel_params,
        name="gather_operand",
    )(spread, cross_own, cross_other, prev_panel)


def product_kernel(got, mine, mine_b, next_z, next_zb, out, cross_pair, stride, prev_rows):
    row = lax.axis_index("prow")
    core = lax.axis_index("pcol") % 2
    half = row % 2
    strided = row // 16
    for k in range(COLS):
        stride[4 * k : 4 * k + 4, :] = got[2 * k + strided, 32:36, :]
        prev_rows[4 * k : 4 * k + 4, :] = got[2 * k + 1 - strided, 32:36, :]
    own = got[pl.ds(16 * core, 16), :32, :].reshape(512, 128)
    other = got[pl.ds(16 - 16 * core, 16), :32, :].reshape(512, 128)
    own_prev = prev_rows[pl.ds(pl.multiple_of(32 * core, 32), 32), :]
    other_prev = prev_rows[pl.ds(pl.multiple_of(32 - 32 * core, 32), 32), :]
    prev = jnp.concatenate([own_prev, other_prev], 0)
    sums = -jnp.sum(got[:, 32:40, :], 0)
    pad = jnp.zeros((4, 128), jnp.float32)
    cross = jnp.concatenate([sums[4:8], pad], 0)
    cross_pair[...] = cross
    for left, right, which in ((mine, mine_b, half), (next_z, next_zb, 1 - half)):
        top = jnp.concatenate([left[256:, :256], left[256:, 256:], right[256:, :256], right[256:, 256:]], 0)
        part = dot(left[:256, :], own) + dot(right[:256, :], other) + dot(top.T, prev)
        part = part.T
        for y in range(YS):
            out[2 * y + which, :16, :] = part[16 * y : 16 * y + 16, :128]
            out[2 * y + which, 16:32, :] = part[16 * y : 16 * y + 16, 128:]
            out[2 * y + which, 32:, :] = cross


def column_product(got, mine, mine_b, next_z, next_zb):
    return pl.pallas_call(
        product_kernel,
        out_shape=(
            jax.ShapeDtypeStruct((16, 40, 128), jnp.float32),
            jax.ShapeDtypeStruct((8, 128), jnp.float32),
            jax.ShapeDtypeStruct((64, 128), jnp.float32),
        ),
        in_specs=[pl.BlockSpec(memory_space=pltpu.VMEM)] * 5,
        out_specs=(pl.BlockSpec(memory_space=pltpu.VMEM),) * 3,
        scratch_shapes=[pltpu.VMEM((64, 128), jnp.float32)],
        compiler_params=kernel_params,
        name="column_product",
    )(got, mine, mine_b, next_z, next_zb)


def diag_kernel(slots, panel, got, cross_pair, stride, fresh_out, out, columns):
    row = lax.axis_index("prow")
    half = row % 2
    y = lax.axis_index("pcol") // 2
    fresh = []
    for h in range(2):
        total = got[h, :32, :]
        for k in range(1, YS):
            total = total + got[2 * k + h, :32, :]
        fresh.append(jnp.concatenate([-total[:16], -total[16:]], 1))
    fresh = jnp.concatenate(fresh, 0)
    fresh_out[0] = fresh
    low, high = factor_halves(slots, panel, row)
    part = dot(fresh[:, :BLK], low) + dot(fresh[:, BLK:], high)
    for k in range(YS):
        block = got[2 * k + half, 32:40, :]
        for who in range(2):
            for h in range(2):
                columns[h, 2 * k + who : 2 * k + who + 1, :] = block[2 * who + h : 2 * who + h + 1]
    rows = jnp.concatenate([stride[pl.ds(lane, 16, stride=4), :] for lane in range(4)], 1)
    own = []
    for h in range(2):
        columns[2 + h, :, :] = jnp.zeros((128, 128), jnp.float32)
        columns[2 + h, :, :16] = columns[h, :16, :].T
        picked = columns[2 + h, pl.ds(pl.multiple_of(16 * y, 16), 16), :]
        own.append(dot(picked[:, :16], rows))
    part = part + jnp.concatenate(own, 0)
    for k in range(ROWS):
        for lane in range(4):
            out[k, lane : lane + 1, :] = part[k : k + 1, 128 * lane : 128 * lane + 128]
        out[k, 4:8, :] = cross_pair[:4, :]


def diag_operand(slot_blocks, panel_blocks, got, cross_pair, stride):
    return pl.pallas_call(
        diag_kernel,
        out_shape=(
            jax.ShapeDtypeStruct((1, 32, 256), jnp.float32),
            jax.ShapeDtypeStruct((ROWS, 8, 128), jnp.float32),
        ),
        in_specs=[pl.BlockSpec(memory_space=pltpu.SMEM)] + [pl.BlockSpec(memory_space=pltpu.VMEM)] * 4,
        out_specs=(pl.BlockSpec(memory_space=pltpu.VMEM),) * 2,
        scratch_shapes=[pltpu.VMEM((4, 128, 128), jnp.float32)],
        compiler_params=kernel_params,
        name="diag_operand",
    )(slot_blocks, panel_blocks, got, cross_pair, stride)


def total_kernel(got, out, keep, give):
    core = lax.axis_index("pcol") % 2
    total = jnp.sum(got[:, :4, :], 0)
    for k in range(ROWS):
        out[k] = total
        for lane in range(2):
            span = slice(128 * lane, 128 * lane + 128)
            first, second = got[k, 4 + lane : 5 + lane, :], got[k, 6 + lane : 7 + lane, :]
            keep[k : k + 1, span] = jnp.where(core == 0, first, second)
            give[k : k + 1, span] = jnp.where(core == 0, second, first)


def total_operand(got):
    return pl.pallas_call(
        total_kernel,
        out_shape=(
            jax.ShapeDtypeStruct((ROWS, 4, 128), jnp.float32),
            jax.ShapeDtypeStruct((32, 256), jnp.float32),
            jax.ShapeDtypeStruct((32, 256), jnp.float32),
        ),
        in_specs=[pl.BlockSpec(memory_space=pltpu.VMEM)],
        out_specs=(pl.BlockSpec(memory_space=pltpu.VMEM),) * 3,
        compiler_params=kernel_params,
        name="total_operand",
    )(got)


def place_columns(core):
    n = lax.broadcasted_iota(jnp.int32, (256, 512), 0)
    target = lax.broadcasted_iota(jnp.int32, (256, 512), 1)
    return (target == 64 * ((n % 128) // 16) + 32 * core + 16 * (n // 128) + n % 16).astype(jnp.float32)


def line_kernel(keep, taken, out):
    core = lax.axis_index("pcol") % 2
    out[0] = dot(keep[...], place_columns(core)) + dot(taken[...], place_columns(1 - core))


def cross_lines(keep, taken):
    return pl.pallas_call(
        line_kernel,
        out_shape=jax.ShapeDtypeStruct((1, 32, 512), jnp.float32),
        in_specs=[pl.BlockSpec(memory_space=pltpu.VMEM)] * 2,
        out_specs=pl.BlockSpec(memory_space=pltpu.VMEM),
        compiler_params=kernel_params,
        name="cross_lines",
    )(keep, taken)


def last_kernel(got, pivot, out):
    for k in range(ROWS):
        for lane in range(4):
            span = slice(128 * lane, 128 * lane + 128)
            out[0, k : k + 1, span] = pivot[0, k : k + 1, span] - got[k, lane : lane + 1, :]


def last_step(got, pivot_inverse):
    return pl.pallas_call(
        last_kernel,
        out_shape=jax.ShapeDtypeStruct((1, 32, 512), jnp.float32),
        in_specs=[pl.BlockSpec(memory_space=pltpu.VMEM)] * 2,
        out_specs=pl.BlockSpec(memory_space=pltpu.VMEM),
        compiler_params=kernel_params,
        name="last_step",
    )(got, pivot_inverse)


def step(pool_inverse, panel_blocks, prev_panel, pivot_inverse, top_column, top_diag, slot_blocks):
    core_swap = [(i, i ^ 1) for i in range(COLS)]
    row_swap = [(i, i ^ 1) for i in range(ROWS)]

    sent = own_piece(slot_blocks, panel_blocks, prev_panel)
    sent, top_column = lax.optimization_barrier((sent, top_column))
    spread = lax.ppermute(sent, ("prow", "pcol"), spread_pairs())

    blocks = jnp.concatenate([pool_inverse, jnp.concatenate([top_column[:16], top_column[16:]], 1)], 0)
    blocks_z = lax.ppermute(blocks, "prow", row_swap)
    blocks_b = lax.ppermute(blocks, "pcol", core_swap)

    cross_own, cross_sent = cross_rows(slot_blocks, panel_blocks, top_column, top_diag, prev_panel)
    cross_other = lax.ppermute(cross_sent, "pcol", core_swap)

    send = gather_operand(spread, cross_own, cross_other, prev_panel)
    got = lax.all_to_all(send, "prow", 0, 0, tiled=True)
    blocks_zb = lax.ppermute(blocks_z, "pcol", core_swap)

    send, cross_pair, stride = column_product(got, blocks, blocks_b, blocks_z, blocks_zb)
    groups = [
        [(x * 8 + 2 * z + h) * COLS + 2 * i + k for i in range(YS) for h in range(2)]
        for x in range(4)
        for z in range(4)
        for k in range(2)
    ]
    got = lax.all_to_all(send, ("prow", "pcol"), 0, 0, tiled=True, axis_index_groups=groups)
    fresh, send = diag_operand(slot_blocks, panel_blocks, got, cross_pair, stride)
    got = lax.all_to_all(send, "prow", 0, 0, tiled=True)
    total, keep, give = total_operand(got)
    got = lax.all_to_all(total, "prow", 0, 0, tiled=True)
    taken = lax.ppermute(give, "pcol", core_swap)
    cross_out = cross_lines(keep, taken)
    return fresh, cross_out, last_step(got, pivot_inverse)


def solution(mesh):
    in_specs = (
        P("prow", "pcol"),
        P(None, "prow", None),
        P(None, "prow", None),
        P(None, "pcol", None),
        P("pcol", "prow"),
        P("pcol", None),
        P(),
    )
    out_specs = (P(None, "pcol", "prow"), P(None, "pcol", None), P(None, "pcol", None))
    return jax.shard_map(step, mesh=mesh, in_specs=in_specs, out_specs=out_specs, check_vma=False)
```

```python
import jax
import jax.numpy as jnp
from jax import lax
from jax.experimental import pallas as pl
from jax.experimental.pallas import tpu as pltpu
from jax.sharding import PartitionSpec as P


BLK = 128
ROWS = 32
COLS = 16
YS = 8

highest = lax.Precision.HIGHEST
kernel_params = pltpu.CompilerParams(vmem_limit_bytes=16 << 20)


def half_of(row):
    return (row // 8) % 2


def spread_pairs():
    pairs = []
    for row in range(ROWS):
        for col in range(COLS):
            y, q, z = row // 4, row % 4, row % 8
            t = (col // 2 - y - 4 + z) % 8
            pairs.append((row * COLS + col, (8 * q + t) * COLS + 2 * y + col % 2))
    return pairs


def select_columns(core):
    source = lax.broadcasted_iota(jnp.int32, (512, 256), 0)
    n = lax.broadcasted_iota(jnp.int32, (512, 256), 1)
    wanted = 64 * ((n % 128) // 16) + 32 * core + 16 * (n // 128) + n % 16
    return (source == wanted).astype(jnp.float32)


def dot(left, right):
    return jnp.dot(left, right, precision=highest, preferred_element_type=jnp.float32)


def piece_kernel(slots, panel, prev, out, ids, buffer, rows, sems):
    row = lax.axis_index("prow")
    col = lax.axis_index("pcol")
    piece = (col // 2 + 16 - row // 4 - 4 + row % 8) % 8
    offset = 32 * (piece % 4)
    copies = [
        pltpu.make_async_copy(panel.at[0, pl.ds(BLK * k + offset, 32), :], buffer.at[k], sems.at[k]) for k in range(2)
    ]
    copies.append(pltpu.make_async_copy(prev.at[0], rows, sems.at[2]))
    copies.append(pltpu.make_async_copy(slots, ids, sems.at[3]))
    for copy in copies:
        copy.start()
    wanted = 2 * row + piece // 4
    columns = select_columns(col % 2)
    for copy in copies:
        copy.wait()
    rolled = pltpu.roll(rows[...], (16 - 4 * (piece // 2)) % 16, 0)
    zero = jnp.zeros((32, 512), jnp.float32)
    chunk = jnp.where(ids[0, 2 * row] == wanted, buffer[0], zero)
    chunk = jnp.where(ids[0, 2 * row + 1] == wanted, buffer[1], chunk)
    out[...] = dot(jnp.concatenate([chunk, rolled[:8]], 0), columns)


def own_piece(slot_blocks, panel_blocks, prev_panel):
    return pl.pallas_call(
        piece_kernel,
        out_shape=jax.ShapeDtypeStruct((40, 256), jnp.float32),
        in_specs=[pl.BlockSpec(memory_space=pltpu.HBM)] * 3,
        out_specs=pl.BlockSpec(memory_space=pltpu.VMEM),
        scratch_shapes=[
            pltpu.SMEM((1, 64), jnp.int32),
            pltpu.VMEM((2, 32, 512), jnp.float32),
            pltpu.VMEM((16, 512), jnp.float32),
            pltpu.SemaphoreType.DMA((4,)),
        ],
        name="own_piece",
    )(slot_blocks, panel_blocks, prev_panel)


def factor_halves(slots, panel, row):
    first, second = panel[0, :BLK, :], panel[0, BLK:, :]
    zero = jnp.zeros_like(first)
    low = jnp.where(slots[0, 2 * row] == 2 * row, first, zero)
    high = jnp.where(slots[0, 2 * row + 1] == 2 * row + 1, second, zero)
    return low, jnp.where(slots[0, 2 * row] == 2 * row + 1, first, high)


def cross_kernel(slots, panel, top_column, top_diag, prev, mine, others):
    row = lax.axis_index("prow")
    core = lax.axis_index("pcol") % 2
    low, high = factor_halves(slots, panel, row)
    diag = pltpu.roll(top_diag[...], (512 - 16 * row) % 512, 1)[:, :16]
    part = dot(top_column[:, :BLK], low) + dot(top_column[:, BLK:], high) + dot(diag, prev[0])
    shifted = jnp.where(core == 0, pltpu.roll(part, 480, 1), pltpu.roll(part, 32, 1))
    both = dot(jnp.concatenate([part, shifted], 0), select_columns(core))
    mine[...] = both[:32]
    others[...] = both[32:]


def cross_rows(slot_blocks, panel_blocks, top_column, top_diag, prev_panel):
    return pl.pallas_call(
        cross_kernel,
        out_shape=(
            jax.ShapeDtypeStruct((32, 256), jnp.float32),
            jax.ShapeDtypeStruct((32, 256), jnp.float32),
        ),
        in_specs=[pl.BlockSpec(memory_space=pltpu.SMEM)] + [pl.BlockSpec(memory_space=pltpu.VMEM)] * 4,
        out_specs=(pl.BlockSpec(memory_space=pltpu.VMEM),) * 2,
        compiler_params=kernel_params,
        name="cross_rows",
    )(slot_blocks, panel_blocks, top_column, top_diag, prev_panel)


def gather_kernel(spread, cross_own, cross_other, prev, out):
    row = lax.axis_index("prow")
    core = lax.axis_index("pcol") % 2
    mine, others = cross_own[...], cross_other[...]
    pair = [jnp.where(core == 0, mine, others), jnp.where(core == 0, others, mine)]
    for k in range(ROWS):
        span = slice(128 * half_of(k), 128 * half_of(k) + 128)
        out[k, :36, :] = spread[:36, span]
        for lane in range(2):
            for who in range(2):
                at = 36 + 2 * who + lane
                out[k, at : at + 1, :] = pair[who][k : k + 1, 128 * lane : 128 * lane + 128]
    for parity in range(2):

        @pl.when(row % 2 == parity)
        def _():
            for k in range(16):
                for lane in range(4):
                    span = slice(128 * lane, 128 * lane + 128)
                    out[16 * parity + k, 32 + lane : 33 + lane, :] = prev[0, k : k + 1, span]


def gather_operand(spread, cross_own, cross_other, prev_panel):
    return pl.pallas_call(
        gather_kernel,
        out_shape=jax.ShapeDtypeStruct((ROWS, 40, 128), jnp.float32),
        in_specs=[pl.BlockSpec(memory_space=pltpu.VMEM)] * 4,
        out_specs=pl.BlockSpec(memory_space=pltpu.VMEM),
        compiler_params=kernel_params,
        name="gather_operand",
    )(spread, cross_own, cross_other, prev_panel)


def product_kernel(got, mine, mine_b, next_x, next_xb, out, cross_pair, stride, prev_rows):
    row = lax.axis_index("prow")
    core = lax.axis_index("pcol") % 2
    half = half_of(row)
    strided = row // 16
    for k in range(COLS):
        stride[4 * k : 4 * k + 4, :] = got[2 * k + strided, 32:36, :]
        prev_rows[4 * k : 4 * k + 4, :] = got[2 * k + 1 - strided, 32:36, :]
    own = got[pl.ds(16 * core, 16), :32, :].reshape(512, 128)
    other = got[pl.ds(16 - 16 * core, 16), :32, :].reshape(512, 128)
    own_prev = prev_rows[pl.ds(pl.multiple_of(32 * core, 32), 32), :]
    other_prev = prev_rows[pl.ds(pl.multiple_of(32 - 32 * core, 32), 32), :]
    prev = jnp.concatenate([own_prev, other_prev], 0)
    sums = -jnp.sum(got[:, 32:40, :], 0)
    pad = jnp.zeros((4, 128), jnp.float32)
    cross = jnp.concatenate([sums[4:8], pad], 0)
    cross_pair[...] = cross
    for left, right, which in ((mine, mine_b, half), (next_x, next_xb, 1 - half)):
        top = jnp.concatenate([left[256:, :256], left[256:, 256:], right[256:, :256], right[256:, 256:]], 0)
        part = dot(left[:256, :], own) + dot(right[:256, :], other) + dot(top.T, prev)
        part = part.T
        for y in range(YS):
            out[2 * y + which, :16, :] = part[16 * y : 16 * y + 16, :128]
            out[2 * y + which, 16:32, :] = part[16 * y : 16 * y + 16, 128:]
            out[2 * y + which, 32:, :] = cross


def column_product(got, mine, mine_b, next_x, next_xb):
    return pl.pallas_call(
        product_kernel,
        out_shape=(
            jax.ShapeDtypeStruct((16, 40, 128), jnp.float32),
            jax.ShapeDtypeStruct((8, 128), jnp.float32),
            jax.ShapeDtypeStruct((64, 128), jnp.float32),
        ),
        in_specs=[pl.BlockSpec(memory_space=pltpu.VMEM)] * 5,
        out_specs=(pl.BlockSpec(memory_space=pltpu.VMEM),) * 3,
        scratch_shapes=[pltpu.VMEM((64, 128), jnp.float32)],
        compiler_params=kernel_params,
        name="column_product",
    )(got, mine, mine_b, next_x, next_xb)


def diag_kernel(slots, panel, got, cross_pair, stride, fresh_out, out, columns):
    row = lax.axis_index("prow")
    half = half_of(row)
    y = lax.axis_index("pcol") // 2
    fresh = []
    for h in range(2):
        total = got[h, :32, :]
        for k in range(1, YS):
            total = total + got[2 * k + h, :32, :]
        fresh.append(jnp.concatenate([-total[:16], -total[16:]], 1))
    fresh = jnp.concatenate(fresh, 0)
    fresh_out[0] = fresh
    low, high = factor_halves(slots, panel, row)
    part = dot(fresh[:, :BLK], low) + dot(fresh[:, BLK:], high)
    for k in range(YS):
        block = got[2 * k + half, 32:40, :]
        for who in range(2):
            for h in range(2):
                columns[h, 2 * k + who : 2 * k + who + 1, :] = block[2 * who + h : 2 * who + h + 1]
    rows = jnp.concatenate([stride[pl.ds(lane, 16, stride=4), :] for lane in range(4)], 1)
    own = []
    for h in range(2):
        columns[2 + h, :, :] = jnp.zeros((128, 128), jnp.float32)
        columns[2 + h, :, :16] = columns[h, :16, :].T
        picked = columns[2 + h, pl.ds(pl.multiple_of(16 * y, 16), 16), :]
        own.append(dot(picked[:, :16], rows))
    part = part + jnp.concatenate(own, 0)
    for k in range(ROWS):
        for lane in range(4):
            out[k, lane : lane + 1, :] = part[k : k + 1, 128 * lane : 128 * lane + 128]
        out[k, 4:8, :] = cross_pair[:4, :]


def diag_operand(slot_blocks, panel_blocks, got, cross_pair, stride):
    return pl.pallas_call(
        diag_kernel,
        out_shape=(
            jax.ShapeDtypeStruct((1, 32, 256), jnp.float32),
            jax.ShapeDtypeStruct((ROWS, 8, 128), jnp.float32),
        ),
        in_specs=[pl.BlockSpec(memory_space=pltpu.SMEM)] + [pl.BlockSpec(memory_space=pltpu.VMEM)] * 4,
        out_specs=(pl.BlockSpec(memory_space=pltpu.VMEM),) * 2,
        scratch_shapes=[pltpu.VMEM((4, 128, 128), jnp.float32)],
        compiler_params=kernel_params,
        name="diag_operand",
    )(slot_blocks, panel_blocks, got, cross_pair, stride)


def total_kernel(got, out, keep, give):
    core = lax.axis_index("pcol") % 2
    total = jnp.sum(got[:, :4, :], 0)
    for k in range(ROWS):
        out[k] = total
        for lane in range(2):
            span = slice(128 * lane, 128 * lane + 128)
            first, second = got[k, 4 + lane : 5 + lane, :], got[k, 6 + lane : 7 + lane, :]
            keep[k : k + 1, span] = jnp.where(core == 0, first, second)
            give[k : k + 1, span] = jnp.where(core == 0, second, first)


def total_operand(got):
    return pl.pallas_call(
        total_kernel,
        out_shape=(
            jax.ShapeDtypeStruct((ROWS, 4, 128), jnp.float32),
            jax.ShapeDtypeStruct((32, 256), jnp.float32),
            jax.ShapeDtypeStruct((32, 256), jnp.float32),
        ),
        in_specs=[pl.BlockSpec(memory_space=pltpu.VMEM)],
        out_specs=(pl.BlockSpec(memory_space=pltpu.VMEM),) * 3,
        compiler_params=kernel_params,
        name="total_operand",
    )(got)


def place_columns(core):
    n = lax.broadcasted_iota(jnp.int32, (256, 512), 0)
    target = lax.broadcasted_iota(jnp.int32, (256, 512), 1)
    return (target == 64 * ((n % 128) // 16) + 32 * core + 16 * (n // 128) + n % 16).astype(jnp.float32)


def line_kernel(keep, taken, out):
    core = lax.axis_index("pcol") % 2
    out[0] = dot(keep[...], place_columns(core)) + dot(taken[...], place_columns(1 - core))


def cross_lines(keep, taken):
    return pl.pallas_call(
        line_kernel,
        out_shape=jax.ShapeDtypeStruct((1, 32, 512), jnp.float32),
        in_specs=[pl.BlockSpec(memory_space=pltpu.VMEM)] * 2,
        out_specs=pl.BlockSpec(memory_space=pltpu.VMEM),
        compiler_params=kernel_params,
        name="cross_lines",
    )(keep, taken)


def last_kernel(got, pivot, out):
    for k in range(ROWS):
        for lane in range(4):
            span = slice(128 * lane, 128 * lane + 128)
            out[0, k : k + 1, span] = pivot[0, k : k + 1, span] - got[k, lane : lane + 1, :]


def last_step(got, pivot_inverse):
    return pl.pallas_call(
        last_kernel,
        out_shape=jax.ShapeDtypeStruct((1, 32, 512), jnp.float32),
        in_specs=[pl.BlockSpec(memory_space=pltpu.VMEM)] * 2,
        out_specs=pl.BlockSpec(memory_space=pltpu.VMEM),
        compiler_params=kernel_params,
        name="last_step",
    )(got, pivot_inverse)


def step(pool_inverse, panel_blocks, prev_panel, pivot_inverse, top_column, top_diag, slot_blocks):
    core_swap = [(i, i ^ 1) for i in range(COLS)]
    row_swap = [(i, i ^ 8) for i in range(ROWS)]

    sent = own_piece(slot_blocks, panel_blocks, prev_panel)
    sent, top_column = lax.optimization_barrier((sent, top_column))
    spread = lax.ppermute(sent, ("prow", "pcol"), spread_pairs())

    blocks = jnp.concatenate([pool_inverse, jnp.concatenate([top_column[:16], top_column[16:]], 1)], 0)
    blocks_x = lax.ppermute(blocks, "prow", row_swap)
    blocks_b = lax.ppermute(blocks, "pcol", core_swap)

    cross_own, cross_sent = cross_rows(slot_blocks, panel_blocks, top_column, top_diag, prev_panel)
    cross_other = lax.ppermute(cross_sent, "pcol", core_swap)

    send = gather_operand(spread, cross_own, cross_other, prev_panel)
    got = lax.all_to_all(send, "prow", 0, 0, tiled=True)
    blocks_xb = lax.ppermute(blocks_x, "pcol", core_swap)

    send, cross_pair, stride = column_product(got, blocks, blocks_b, blocks_x, blocks_xb)
    groups = [
        [((2 * x + h) * 8 + z) * COLS + 2 * i + k for i in range(YS) for h in range(2)]
        for x in range(2)
        for z in range(8)
        for k in range(2)
    ]
    got = lax.all_to_all(send, ("prow", "pcol"), 0, 0, tiled=True, axis_index_groups=groups)
    fresh, send = diag_operand(slot_blocks, panel_blocks, got, cross_pair, stride)
    got = lax.all_to_all(send, "prow", 0, 0, tiled=True)
    total, keep, give = total_operand(got)
    got = lax.all_to_all(total, "prow", 0, 0, tiled=True)
    taken = lax.ppermute(give, "pcol", core_swap)
    cross_out = cross_lines(keep, taken)
    return fresh, cross_out, last_step(got, pivot_inverse)


def solution(mesh):
    in_specs = (
        P("prow", "pcol"),
        P(None, "prow", None),
        P(None, "prow", None),
        P(None, "pcol", None),
        P("pcol", "prow"),
        P("pcol", None),
        P(),
    )
    out_specs = (P(None, "pcol", "prow"), P(None, "pcol", None), P(None, "pcol", None))
    return jax.shard_map(step, mesh=mesh, in_specs=in_specs, out_specs=out_specs, check_vma=False)
```

```python
import jax
import jax.numpy as jnp
from jax import lax
from jax.experimental import pallas as pl
from jax.experimental.pallas import tpu as pltpu
from jax.sharding import PartitionSpec as P


BLK = 128
ROWS = 32
COLS = 16
YS = 8


highest = lax.Precision.HIGHEST
kernel_params = pltpu.CompilerParams(vmem_limit_bytes=16 << 20)


def half_of(row):
    return row % 2


def spread_pairs():
    pairs = []
    for row in range(ROWS):
        for col in range(COLS):
            y, q, z = row // 4, row % 4, row % 8
            t = (col // 2 - y - 4 + z) % 8
            pairs.append((row * COLS + col, (8 * q + t) * COLS + 2 * y + col % 2))
    return pairs


def select_columns(core):
    source = lax.broadcasted_iota(jnp.int32, (512, 256), 0)
    n = lax.broadcasted_iota(jnp.int32, (512, 256), 1)
    wanted = 64 * ((n % 128) // 16) + 32 * core + 16 * (n // 128) + n % 16
    return (source == wanted).astype(jnp.float32)


def dot(left, right):
    return jnp.dot(left, right, precision=highest, preferred_element_type=jnp.float32)


def piece_kernel(slots, panel, prev, out, ids, buffer, rows, sems):
    row = lax.axis_index("prow")
    col = lax.axis_index("pcol")
    target = (col // 2 + 16 - row // 4 - 4 + row % 8) % 8
    copies = [
        pltpu.make_async_copy(panel.at[0], buffer, sems.at[0]),
        pltpu.make_async_copy(prev.at[0], rows, sems.at[1]),
        pltpu.make_async_copy(slots, ids, sems.at[2]),
    ]
    for copy in copies:
        copy.start()
    source = lax.broadcasted_iota(jnp.int32, (512, 128), 0)
    n = lax.broadcasted_iota(jnp.int32, (512, 128), 1)
    wanted = 64 * (n // 16) + 32 * (col % 2) + 16 * half_of(target) + n % 16
    columns = (source == wanted).astype(jnp.float32)
    for copy in copies:
        copy.wait()
    picked = dot(buffer[...], columns)
    zero = jnp.zeros((BLK, 128), jnp.float32)
    low = jnp.where(ids[0, 2 * row] == 2 * row, picked[:BLK], zero)
    high = jnp.where(ids[0, 2 * row + 1] == 2 * row + 1, picked[BLK:], zero)
    out[:BLK, :] = low
    out[BLK : 2 * BLK, :] = jnp.where(ids[0, 2 * row] == 2 * row + 1, picked[:BLK], high)
    out[2 * BLK :, :] = dot(rows[...], columns)


def own_piece(slot_blocks, panel_blocks, prev_panel):
    return pl.pallas_call(
        piece_kernel,
        out_shape=jax.ShapeDtypeStruct((272, 128), jnp.float32),
        in_specs=[pl.BlockSpec(memory_space=pltpu.HBM)] * 3,
        out_specs=pl.BlockSpec(memory_space=pltpu.VMEM),
        scratch_shapes=[
            pltpu.SMEM((1, 64), jnp.int32),
            pltpu.VMEM((256, 512), jnp.float32),
            pltpu.VMEM((16, 512), jnp.float32),
            pltpu.SemaphoreType.DMA((3,)),
        ],
        name="own_piece",
    )(slot_blocks, panel_blocks, prev_panel)


def factor_halves(slots, panel, row):
    first, second = panel[0, :BLK, :], panel[0, BLK:, :]
    zero = jnp.zeros_like(first)
    low = jnp.where(slots[0, 2 * row] == 2 * row, first, zero)
    high = jnp.where(slots[0, 2 * row + 1] == 2 * row + 1, second, zero)
    return low, jnp.where(slots[0, 2 * row] == 2 * row + 1, first, high)


def cross_kernel(slots, panel, top_column, top_diag, prev, mine, others):
    row = lax.axis_index("prow")
    core = lax.axis_index("pcol") % 2
    low, high = factor_halves(slots, panel, row)
    diag = pltpu.roll(top_diag[...], (512 - 16 * row) % 512, 1)[:, :16]
    part = dot(top_column[:, :BLK], low) + dot(top_column[:, BLK:], high) + dot(diag, prev[0])
    shifted = jnp.where(core == 0, pltpu.roll(part, 480, 1), pltpu.roll(part, 32, 1))
    both = dot(jnp.concatenate([part, shifted], 0), select_columns(core))
    mine[...] = both[:32]
    others[...] = both[32:]


def cross_rows(slot_blocks, panel_blocks, top_column, top_diag, prev_panel):
    return pl.pallas_call(
        cross_kernel,
        out_shape=(
            jax.ShapeDtypeStruct((32, 256), jnp.float32),
            jax.ShapeDtypeStruct((32, 256), jnp.float32),
        ),
        in_specs=[pl.BlockSpec(memory_space=pltpu.SMEM)] + [pl.BlockSpec(memory_space=pltpu.VMEM)] * 4,
        out_specs=(pl.BlockSpec(memory_space=pltpu.VMEM),) * 2,
        compiler_params=kernel_params,
        name="cross_rows",
    )(slot_blocks, panel_blocks, top_column, top_diag, prev_panel)


def rows_kernel(cross_own, cross_other, prev, out):
    core = lax.axis_index("pcol") % 2
    mine, others = cross_own[...], cross_other[...]
    pair = [jnp.where(core == 0, mine, others), jnp.where(core == 0, others, mine)]
    for k in range(ROWS):
        for lane in range(4):
            span = slice(128 * lane, 128 * lane + 128)
            out[k, lane : lane + 1, :] = prev[0, k % 16 : k % 16 + 1, span]
            part = pair[lane // 2][k : k + 1, 128 * (lane % 2) : 128 * (lane % 2) + 128]
            out[k, 4 + lane : 5 + lane, :] = part


def rows_operand(cross_own, cross_other, prev_panel):
    return pl.pallas_call(
        rows_kernel,
        out_shape=jax.ShapeDtypeStruct((ROWS, 8, 128), jnp.float32),
        in_specs=[pl.BlockSpec(memory_space=pltpu.VMEM)] * 3,
        out_specs=pl.BlockSpec(memory_space=pltpu.VMEM),
        compiler_params=kernel_params,
        name="rows_operand",
    )(cross_own, cross_other, prev_panel)


def product_kernel(own0, from1, from3, from2, rows, mine, mine_b, next_z, next_zb, out, cross_pair, stride, got):
    row = lax.axis_index("prow")
    core = lax.axis_index("pcol") % 2
    half = half_of(row)
    for shift, part in ((0, own0), (1, from1), (3, from3), (2, from2)):
        got[(row // 8 + 4 - shift) % 4] = part[...]
    for k in range(COLS):
        stride[4 * k : 4 * k + 4, :] = rows[2 * k + row // 16, :4, :]
    own = got[pl.ds(2 * core, 2), : 2 * BLK, :].reshape(512, 128)
    other = got[pl.ds(2 - 2 * core, 2), : 2 * BLK, :].reshape(512, 128)
    own_prev = got[pl.ds(2 * core, 2), 2 * BLK :, :].reshape(32, 128)
    other_prev = got[pl.ds(2 - 2 * core, 2), 2 * BLK :, :].reshape(32, 128)
    prev = jnp.concatenate([own_prev, other_prev], 0)
    sums = -jnp.sum(rows[...], 0)
    pad = jnp.zeros((4, 128), jnp.float32)
    cross = jnp.concatenate([sums[4:8], pad], 0)
    cross_pair[...] = cross
    for left, right, which in ((mine, mine_b, half), (next_z, next_zb, 1 - half)):
        top = jnp.concatenate([left[256:, :256], left[256:, 256:], right[256:, :256], right[256:, 256:]], 0)
        part = dot(left[:256, :], own) + dot(right[:256, :], other) + dot(top.T, prev)
        part = part.T
        for y in range(YS):
            out[2 * y + which, :16, :] = part[16 * y : 16 * y + 16, :128]
            out[2 * y + which, 16:32, :] = part[16 * y : 16 * y + 16, 128:]
            out[2 * y + which, 32:, :] = cross


def column_product(own0, from1, from3, from2, rows, mine, mine_b, next_z, next_zb):
    return pl.pallas_call(
        product_kernel,
        out_shape=(
            jax.ShapeDtypeStruct((16, 40, 128), jnp.float32),
            jax.ShapeDtypeStruct((8, 128), jnp.float32),
            jax.ShapeDtypeStruct((64, 128), jnp.float32),
        ),
        in_specs=[pl.BlockSpec(memory_space=pltpu.VMEM)] * 9,
        out_specs=(pl.BlockSpec(memory_space=pltpu.VMEM),) * 3,
        scratch_shapes=[pltpu.VMEM((4, 272, 128), jnp.float32)],
        compiler_params=kernel_params,
        name="column_product",
    )(own0, from1, from3, from2, rows, mine, mine_b, next_z, next_zb)


def diag_kernel(slots, panel, got, cross_pair, stride, fresh_out, out, columns):
    row = lax.axis_index("prow")
    half = half_of(row)
    y = lax.axis_index("pcol") // 2
    fresh = []
    for h in range(2):
        total = got[h, :32, :]
        for k in range(1, YS):
            total = total + got[2 * k + h, :32, :]
        fresh.append(jnp.concatenate([-total[:16], -total[16:]], 1))
    fresh = jnp.concatenate(fresh, 0)
    fresh_out[0] = fresh
    low, high = factor_halves(slots, panel, row)
    part = dot(fresh[:, :BLK], low) + dot(fresh[:, BLK:], high)
    for k in range(YS):
        block = got[2 * k + half, 32:40, :]
        for who in range(2):
            for h in range(2):
                columns[h, 2 * k + who : 2 * k + who + 1, :] = block[2 * who + h : 2 * who + h + 1]
    rows = jnp.concatenate([stride[pl.ds(lane, 16, stride=4), :] for lane in range(4)], 1)
    own = []
    for h in range(2):
        columns[2 + h, :, :] = jnp.zeros((128, 128), jnp.float32)
        columns[2 + h, :, :16] = columns[h, :16, :].T
        picked = columns[2 + h, pl.ds(pl.multiple_of(16 * y, 16), 16), :]
        own.append(dot(picked[:, :16], rows))
    part = part + jnp.concatenate(own, 0)
    for k in range(ROWS):
        for lane in range(4):
            out[k, lane : lane + 1, :] = part[k : k + 1, 128 * lane : 128 * lane + 128]
        out[k, 4:8, :] = cross_pair[:4, :]


def diag_operand(slot_blocks, panel_blocks, got, cross_pair, stride):
    return pl.pallas_call(
        diag_kernel,
        out_shape=(
            jax.ShapeDtypeStruct((1, 32, 256), jnp.float32),
            jax.ShapeDtypeStruct((ROWS, 8, 128), jnp.float32),
        ),
        in_specs=[pl.BlockSpec(memory_space=pltpu.SMEM)] + [pl.BlockSpec(memory_space=pltpu.VMEM)] * 4,
        out_specs=(pl.BlockSpec(memory_space=pltpu.VMEM),) * 2,
        scratch_shapes=[pltpu.VMEM((4, 128, 128), jnp.float32)],
        compiler_params=kernel_params,
        name="diag_operand",
    )(slot_blocks, panel_blocks, got, cross_pair, stride)


def total_kernel(got, out, keep, give):
    core = lax.axis_index("pcol") % 2
    total = jnp.sum(got[:, :4, :], 0)
    for k in range(ROWS):
        out[k] = total
        for lane in range(2):
            span = slice(128 * lane, 128 * lane + 128)
            first, second = got[k, 4 + lane : 5 + lane, :], got[k, 6 + lane : 7 + lane, :]
            keep[k : k + 1, span] = jnp.where(core == 0, first, second)
            give[k : k + 1, span] = jnp.where(core == 0, second, first)


def total_operand(got):
    return pl.pallas_call(
        total_kernel,
        out_shape=(
            jax.ShapeDtypeStruct((ROWS, 4, 128), jnp.float32),
            jax.ShapeDtypeStruct((32, 256), jnp.float32),
            jax.ShapeDtypeStruct((32, 256), jnp.float32),
        ),
        in_specs=[pl.BlockSpec(memory_space=pltpu.VMEM)],
        out_specs=(pl.BlockSpec(memory_space=pltpu.VMEM),) * 3,
        compiler_params=kernel_params,
        name="total_operand",
    )(got)


def place_columns(core):
    n = lax.broadcasted_iota(jnp.int32, (256, 512), 0)
    target = lax.broadcasted_iota(jnp.int32, (256, 512), 1)
    return (target == 64 * ((n % 128) // 16) + 32 * core + 16 * (n // 128) + n % 16).astype(jnp.float32)


def line_kernel(keep, taken, out):
    core = lax.axis_index("pcol") % 2
    out[0] = dot(keep[...], place_columns(core)) + dot(taken[...], place_columns(1 - core))


def cross_lines(keep, taken):
    return pl.pallas_call(
        line_kernel,
        out_shape=jax.ShapeDtypeStruct((1, 32, 512), jnp.float32),
        in_specs=[pl.BlockSpec(memory_space=pltpu.VMEM)] * 2,
        out_specs=pl.BlockSpec(memory_space=pltpu.VMEM),
        compiler_params=kernel_params,
        name="cross_lines",
    )(keep, taken)


def last_kernel(got, pivot, out):
    for k in range(ROWS):
        for lane in range(4):
            span = slice(128 * lane, 128 * lane + 128)
            out[0, k : k + 1, span] = pivot[0, k : k + 1, span] - got[k, lane : lane + 1, :]


def last_step(got, pivot_inverse):
    return pl.pallas_call(
        last_kernel,
        out_shape=jax.ShapeDtypeStruct((1, 32, 512), jnp.float32),
        in_specs=[pl.BlockSpec(memory_space=pltpu.VMEM)] * 2,
        out_specs=pl.BlockSpec(memory_space=pltpu.VMEM),
        compiler_params=kernel_params,
        name="last_step",
    )(got, pivot_inverse)


def step(pool_inverse, panel_blocks, prev_panel, pivot_inverse, top_column, top_diag, slot_blocks):
    core_swap = [(i, i ^ 1) for i in range(COLS)]
    row_swap = [(i, i ^ 1) for i in range(ROWS)]

    sent = own_piece(slot_blocks, panel_blocks, prev_panel)
    sent, top_column = lax.optimization_barrier((sent, top_column))
    spread = lax.ppermute(sent, ("prow", "pcol"), spread_pairs())

    blocks = jnp.concatenate([pool_inverse, jnp.concatenate([top_column[:16], top_column[16:]], 1)], 0)
    blocks_z = lax.ppermute(blocks, "prow", row_swap)
    blocks_b = lax.ppermute(blocks, "pcol", core_swap)

    cross_own, cross_sent = cross_rows(slot_blocks, panel_blocks, top_column, top_diag, prev_panel)
    cross_other = lax.ppermute(cross_sent, "pcol", core_swap)

    rows = lax.all_to_all(rows_operand(cross_own, cross_other, prev_panel), "prow", 0, 0, tiled=True)
    got = [spread]
    for shift in (1, 3, 2):
        got.append(lax.ppermute(spread, "prow", [(i, (i + 8 * shift) % ROWS) for i in range(ROWS)]))
    blocks_zb = lax.ppermute(blocks_z, "pcol", core_swap)

    send, cross_pair, stride = column_product(*got, rows, blocks, blocks_b, blocks_z, blocks_zb)
    groups = [
        [(x * 8 + 2 * z + h) * COLS + 2 * i + k for i in range(YS) for h in range(2)]
        for x in range(4)
        for z in range(4)
        for k in range(2)
    ]
    got = lax.all_to_all(send, ("prow", "pcol"), 0, 0, tiled=True, axis_index_groups=groups)
    fresh, send = diag_operand(slot_blocks, panel_blocks, got, cross_pair, stride)
    got = lax.all_to_all(send, "prow", 0, 0, tiled=True)
    total, keep, give = total_operand(got)
    got = lax.all_to_all(total, "prow", 0, 0, tiled=True)
    taken = lax.ppermute(give, "pcol", core_swap)
    cross_out = cross_lines(keep, taken)
    return fresh, cross_out, last_step(got, pivot_inverse)


def solution(mesh):
    in_specs = (
        P("prow", "pcol"),
        P(None, "prow", None),
        P(None, "prow", None),
        P(None, "pcol", None),
        P("pcol", "prow"),
        P("pcol", None),
        P(),
    )
    out_specs = (P(None, "pcol", "prow"), P(None, "pcol", None), P(None, "pcol", None))
    return jax.shard_map(step, mesh=mesh, in_specs=in_specs, out_specs=out_specs, check_vma=False)
```

```python
import jax
import jax.numpy as jnp
from jax import lax
from jax.experimental import pallas as pl
from jax.experimental.pallas import tpu as pltpu
from jax.sharding import PartitionSpec as P


BLK = 128
ROWS = 32
COLS = 16
YS = 8

highest = lax.Precision.HIGHEST
kernel_params = pltpu.CompilerParams(vmem_limit_bytes=16 << 20)


def half_of(row):
    return (row // 8) % 2


def spread_pairs():
    pairs = []
    for row in range(ROWS):
        for col in range(COLS):
            y, q, z = row // 4, row % 4, row % 8
            t = (col // 2 - y - 4 + z) % 8
            pairs.append((row * COLS + col, (8 * q + t) * COLS + 2 * y + col % 2))
    return pairs


def select_columns(core):
    source = lax.broadcasted_iota(jnp.int32, (512, 256), 0)
    n = lax.broadcasted_iota(jnp.int32, (512, 256), 1)
    wanted = 64 * ((n % 128) // 16) + 32 * core + 16 * (n // 128) + n % 16
    return (source == wanted).astype(jnp.float32)


def dot(left, right):
    return jnp.dot(left, right, precision=highest, preferred_element_type=jnp.float32)


def piece_kernel(slots, panel, prev, out, ids, buffer, rows, sems):
    row = lax.axis_index("prow")
    col = lax.axis_index("pcol")
    piece = (col // 2 + 16 - row // 4 - 4 + row % 8) % 8
    offset = 32 * (piece % 4)
    copies = [
        pltpu.make_async_copy(panel.at[0, pl.ds(BLK * k + offset, 32), :], buffer.at[k], sems.at[k]) for k in range(2)
    ]
    copies.append(pltpu.make_async_copy(prev.at[0], rows, sems.at[2]))
    copies.append(pltpu.make_async_copy(slots, ids, sems.at[3]))
    for copy in copies:
        copy.start()
    wanted = 2 * row + piece // 4
    columns = select_columns(col % 2)
    for copy in copies:
        copy.wait()
    rolled = pltpu.roll(rows[...], (16 - 4 * (piece // 2)) % 16, 0)
    zero = jnp.zeros((32, 512), jnp.float32)
    chunk = jnp.where(ids[0, 2 * row] == wanted, buffer[0], zero)
    chunk = jnp.where(ids[0, 2 * row + 1] == wanted, buffer[1], chunk)
    out[...] = dot(jnp.concatenate([chunk, rolled[:8]], 0), columns)


def own_piece(slot_blocks, panel_blocks, prev_panel):
    return pl.pallas_call(
        piece_kernel,
        out_shape=jax.ShapeDtypeStruct((40, 256), jnp.float32),
        in_specs=[pl.BlockSpec(memory_space=pltpu.HBM)] * 3,
        out_specs=pl.BlockSpec(memory_space=pltpu.VMEM),
        scratch_shapes=[
            pltpu.SMEM((1, 64), jnp.int32),
            pltpu.VMEM((2, 32, 512), jnp.float32),
            pltpu.VMEM((16, 512), jnp.float32),
            pltpu.SemaphoreType.DMA((4,)),
        ],
        name="own_piece",
    )(slot_blocks, panel_blocks, prev_panel)


def factor_halves(slots, panel, row):
    first, second = panel[0, :BLK, :], panel[0, BLK:, :]
    zero = jnp.zeros_like(first)
    low = jnp.where(slots[0, 2 * row] == 2 * row, first, zero)
    high = jnp.where(slots[0, 2 * row + 1] == 2 * row + 1, second, zero)
    return low, jnp.where(slots[0, 2 * row] == 2 * row + 1, first, high)


def cross_kernel(slots, panel, top_column, top_diag, prev, mine, others):
    row = lax.axis_index("prow")
    core = lax.axis_index("pcol") % 2
    low, high = factor_halves(slots, panel, row)
    diag = pltpu.roll(top_diag[...], (512 - 16 * row) % 512, 1)[:, :16]
    part = dot(top_column[:, :BLK], low) + dot(top_column[:, BLK:], high) + dot(diag, prev[0])
    shifted = jnp.where(core == 0, pltpu.roll(part, 480, 1), pltpu.roll(part, 32, 1))
    both = dot(jnp.concatenate([part, shifted], 0), select_columns(core))
    mine[...] = both[:32]
    others[...] = both[32:]


def cross_rows(slot_blocks, panel_blocks, top_column, top_diag, prev_panel):
    return pl.pallas_call(
        cross_kernel,
        out_shape=(
            jax.ShapeDtypeStruct((32, 256), jnp.float32),
            jax.ShapeDtypeStruct((32, 256), jnp.float32),
        ),
        in_specs=[pl.BlockSpec(memory_space=pltpu.SMEM)] + [pl.BlockSpec(memory_space=pltpu.VMEM)] * 4,
        out_specs=(pl.BlockSpec(memory_space=pltpu.VMEM),) * 2,
        compiler_params=kernel_params,
        name="cross_rows",
    )(slot_blocks, panel_blocks, top_column, top_diag, prev_panel)


def gather_kernel(spread, cross_own, cross_other, prev, out):
    row = lax.axis_index("prow")
    core = lax.axis_index("pcol") % 2
    mine, others = cross_own[...], cross_other[...]
    pair = [jnp.where(core == 0, mine, others), jnp.where(core == 0, others, mine)]
    for k in range(ROWS):
        span = slice(128 * half_of(k), 128 * half_of(k) + 128)
        out[k, :36, :] = spread[:36, span]
        for lane in range(2):
            for who in range(2):
                at = 36 + 2 * who + lane
                out[k, at : at + 1, :] = pair[who][k : k + 1, 128 * lane : 128 * lane + 128]
    for parity in range(2):

        @pl.when(row % 2 == parity)
        def _():
            for k in range(16):
                for lane in range(4):
                    span = slice(128 * lane, 128 * lane + 128)
                    out[16 * parity + k, 32 + lane : 33 + lane, :] = prev[0, k : k + 1, span]


def gather_operand(spread, cross_own, cross_other, prev_panel):
    return pl.pallas_call(
        gather_kernel,
        out_shape=jax.ShapeDtypeStruct((ROWS, 40, 128), jnp.float32),
        in_specs=[pl.BlockSpec(memory_space=pltpu.VMEM)] * 4,
        out_specs=pl.BlockSpec(memory_space=pltpu.VMEM),
        compiler_params=kernel_params,
        name="gather_operand",
    )(spread, cross_own, cross_other, prev_panel)


def product_kernel(got, mine, mine_b, next_x, next_xb, out, cross_pair, stride, prev_rows):
    row = lax.axis_index("prow")
    core = lax.axis_index("pcol") % 2
    half = half_of(row)
    strided = row // 16
    for k in range(COLS):
        stride[4 * k : 4 * k + 4, :] = got[2 * k + strided, 32:36, :]
        prev_rows[4 * k : 4 * k + 4, :] = got[2 * k + 1 - strided, 32:36, :]
    own = got[pl.ds(16 * core, 16), :32, :].reshape(512, 128)
    other = got[pl.ds(16 - 16 * core, 16), :32, :].reshape(512, 128)
    own_prev = prev_rows[pl.ds(pl.multiple_of(32 * core, 32), 32), :]
    other_prev = prev_rows[pl.ds(pl.multiple_of(32 - 32 * core, 32), 32), :]
    prev = jnp.concatenate([own_prev, other_prev], 0)
    sums = -jnp.sum(got[:, 32:40, :], 0)
    pad = jnp.zeros((4, 128), jnp.float32)
    cross = jnp.concatenate([sums[4:8], pad], 0)
    cross_pair[...] = cross
    for left, right, which in ((mine, mine_b, half), (next_x, next_xb, 1 - half)):
        top = jnp.concatenate([left[256:, :256], left[256:, 256:], right[256:, :256], right[256:, 256:]], 0)
        part = dot(left[:256, :], own) + dot(right[:256, :], other) + dot(top.T, prev)
        part = part.T
        for y in range(YS):
            out[2 * y + which, :16, :] = part[16 * y : 16 * y + 16, :128]
            out[2 * y + which, 16:32, :] = part[16 * y : 16 * y + 16, 128:]
            out[2 * y + which, 32:, :] = cross


def column_product(got, mine, mine_b, next_x, next_xb):
    return pl.pallas_call(
        product_kernel,
        out_shape=(
            jax.ShapeDtypeStruct((16, 40, 128), jnp.float32),
            jax.ShapeDtypeStruct((8, 128), jnp.float32),
            jax.ShapeDtypeStruct((64, 128), jnp.float32),
        ),
        in_specs=[pl.BlockSpec(memory_space=pltpu.VMEM)] * 5,
        out_specs=(pl.BlockSpec(memory_space=pltpu.VMEM),) * 3,
        scratch_shapes=[pltpu.VMEM((64, 128), jnp.float32)],
        compiler_params=kernel_params,
        name="column_product",
    )(got, mine, mine_b, next_x, next_xb)


def diag_kernel(slots, panel, got, cross_pair, stride, fresh_out, out, columns):
    row = lax.axis_index("prow")
    half = half_of(row)
    y = lax.axis_index("pcol") // 2
    fresh = []
    for h in range(2):
        total = got[h, :32, :]
        for k in range(1, YS):
            total = total + got[2 * k + h, :32, :]
        fresh.append(jnp.concatenate([-total[:16], -total[16:]], 1))
    fresh = jnp.concatenate(fresh, 0)
    fresh_out[0] = fresh
    low, high = factor_halves(slots, panel, row)
    part = dot(fresh[:, :BLK], low) + dot(fresh[:, BLK:], high)
    for k in range(YS):
        block = got[2 * k + half, 32:40, :]
        for who in range(2):
            for h in range(2):
                columns[h, 2 * k + who : 2 * k + who + 1, :] = block[2 * who + h : 2 * who + h + 1]
    rows = jnp.concatenate([stride[pl.ds(lane, 16, stride=4), :] for lane in range(4)], 1)
    own = []
    for h in range(2):
        columns[2 + h, :, :] = jnp.zeros((128, 128), jnp.float32)
        columns[2 + h, :, :16] = columns[h, :16, :].T
        picked = columns[2 + h, pl.ds(pl.multiple_of(16 * y, 16), 16), :]
        own.append(dot(picked[:, :16], rows))
    part = part + jnp.concatenate(own, 0)
    for x in range(4):
        for lane in range(4):
            out[x, 8 * lane : 8 * lane + 8, :] = part[8 * x : 8 * x + 8, 128 * lane : 128 * lane + 128]
        out[x, 32:, :] = cross_pair[...]


def diag_operand(slot_blocks, panel_blocks, got, cross_pair, stride):
    return pl.pallas_call(
        diag_kernel,
        out_shape=(
            jax.ShapeDtypeStruct((1, 32, 256), jnp.float32),
            jax.ShapeDtypeStruct((4, 40, 128), jnp.float32),
        ),
        in_specs=[pl.BlockSpec(memory_space=pltpu.SMEM)] + [pl.BlockSpec(memory_space=pltpu.VMEM)] * 4,
        out_specs=(pl.BlockSpec(memory_space=pltpu.VMEM),) * 2,
        scratch_shapes=[pltpu.VMEM((4, 128, 128), jnp.float32)],
        compiler_params=kernel_params,
        name="diag_operand",
    )(slot_blocks, panel_blocks, got, cross_pair, stride)


def middle_kernel(got, out):
    total = jnp.sum(got[:, :32, :], 0)
    for z in range(8):
        out[z, :32, :] = total
        for x in range(4):
            out[z, 32 + 4 * x : 36 + 4 * x, :] = got[x, 32:36, :]


def middle_operand(got):
    return pl.pallas_call(
        middle_kernel,
        out_shape=jax.ShapeDtypeStruct((8, 48, 128), jnp.float32),
        in_specs=[pl.BlockSpec(memory_space=pltpu.VMEM)],
        out_specs=pl.BlockSpec(memory_space=pltpu.VMEM),
        compiler_params=kernel_params,
        name="middle_operand",
    )(got)


def total_kernel(got, out, keep, give):
    core = lax.axis_index("pcol") % 2
    total = jnp.sum(got[:, :32, :], 0)
    for x in range(4):
        out[x] = total
    for k in range(ROWS):
        at = 32 + 4 * (k // 8)
        for lane in range(2):
            span = slice(128 * lane, 128 * lane + 128)
            first = got[k % 8, at + lane : at + lane + 1, :]
            second = got[k % 8, at + lane + 2 : at + lane + 3, :]
            keep[k : k + 1, span] = jnp.where(core == 0, first, second)
            give[k : k + 1, span] = jnp.where(core == 0, second, first)


def total_operand(got):
    return pl.pallas_call(
        total_kernel,
        out_shape=(
            jax.ShapeDtypeStruct((4, 32, 128), jnp.float32),
            jax.ShapeDtypeStruct((32, 256), jnp.float32),
            jax.ShapeDtypeStruct((32, 256), jnp.float32),
        ),
        in_specs=[pl.BlockSpec(memory_space=pltpu.VMEM)],
        out_specs=(pl.BlockSpec(memory_space=pltpu.VMEM),) * 3,
        compiler_params=kernel_params,
        name="total_operand",
    )(got)


def place_columns(core):
    n = lax.broadcasted_iota(jnp.int32, (256, 512), 0)
    target = lax.broadcasted_iota(jnp.int32, (256, 512), 1)
    return (target == 64 * ((n % 128) // 16) + 32 * core + 16 * (n // 128) + n % 16).astype(jnp.float32)


def line_kernel(keep, taken, out):
    core = lax.axis_index("pcol") % 2
    out[0] = dot(keep[...], place_columns(core)) + dot(taken[...], place_columns(1 - core))


def cross_lines(keep, taken):
    return pl.pallas_call(
        line_kernel,
        out_shape=jax.ShapeDtypeStruct((1, 32, 512), jnp.float32),
        in_specs=[pl.BlockSpec(memory_space=pltpu.VMEM)] * 2,
        out_specs=pl.BlockSpec(memory_space=pltpu.VMEM),
        compiler_params=kernel_params,
        name="cross_lines",
    )(keep, taken)


def last_kernel(got, pivot, out):
    for x in range(4):
        for lane in range(4):
            rows, span = slice(8 * x, 8 * x + 8), slice(128 * lane, 128 * lane + 128)
            out[0, rows, span] = pivot[0, rows, span] - got[x, 8 * lane : 8 * lane + 8, :]


def last_step(got, pivot_inverse):
    return pl.pallas_call(
        last_kernel,
        out_shape=jax.ShapeDtypeStruct((1, 32, 512), jnp.float32),
        in_specs=[pl.BlockSpec(memory_space=pltpu.VMEM)] * 2,
        out_specs=pl.BlockSpec(memory_space=pltpu.VMEM),
        compiler_params=kernel_params,
        name="last_step",
    )(got, pivot_inverse)


def step(pool_inverse, panel_blocks, prev_panel, pivot_inverse, top_column, top_diag, slot_blocks):
    core_swap = [(i, i ^ 1) for i in range(COLS)]
    row_swap = [(i, i ^ 8) for i in range(ROWS)]

    sent = own_piece(slot_blocks, panel_blocks, prev_panel)
    sent, top_column = lax.optimization_barrier((sent, top_column))
    spread = lax.ppermute(sent, ("prow", "pcol"), spread_pairs())

    blocks = jnp.concatenate([pool_inverse, jnp.concatenate([top_column[:16], top_column[16:]], 1)], 0)
    blocks_x = lax.ppermute(blocks, "prow", row_swap)
    blocks_b = lax.ppermute(blocks, "pcol", core_swap)

    cross_own, cross_sent = cross_rows(slot_blocks, panel_blocks, top_column, top_diag, prev_panel)
    cross_other = lax.ppermute(cross_sent, "pcol", core_swap)

    send = gather_operand(spread, cross_own, cross_other, prev_panel)
    got = lax.all_to_all(send, "prow", 0, 0, tiled=True)
    blocks_xb = lax.ppermute(blocks_x, "pcol", core_swap)

    send, cross_pair, stride = column_product(got, blocks, blocks_b, blocks_x, blocks_xb)
    groups = [
        [((2 * x + h) * 8 + z) * COLS + 2 * i + k for i in range(YS) for h in range(2)]
        for x in range(2)
        for z in range(8)
        for k in range(2)
    ]
    got = lax.all_to_all(send, ("prow", "pcol"), 0, 0, tiled=True, axis_index_groups=groups)
    fresh, send = diag_operand(slot_blocks, panel_blocks, got, cross_pair, stride)
    along_x = [[x * 8 + z for x in range(4)] for z in range(8)]
    along_z = [[x * 8 + z for z in range(8)] for x in range(4)]
    got = lax.all_to_all(send, "prow", 0, 0, tiled=True, axis_index_groups=along_x)
    got = lax.all_to_all(middle_operand(got), "prow", 0, 0, tiled=True, axis_index_groups=along_z)
    total, keep, give = total_operand(got)
    got = lax.all_to_all(total, "prow", 0, 0, tiled=True, axis_index_groups=along_x)
    taken = lax.ppermute(give, "pcol", core_swap)
    cross_out = cross_lines(keep, taken)
    return fresh, cross_out, last_step(got, pivot_inverse)


def solution(mesh):
    in_specs = (
        P("prow", "pcol"),
        P(None, "prow", None),
        P(None, "prow", None),
        P(None, "pcol", None),
        P("pcol", "prow"),
        P("pcol", None),
        P(),
    )
    out_specs = (P(None, "pcol", "prow"), P(None, "pcol", None), P(None, "pcol", None))
    return jax.shard_map(step, mesh=mesh, in_specs=in_specs, out_specs=out_specs, check_vma=False)
```

```python
import jax
import jax.numpy as jnp
from jax import lax
from jax.experimental import pallas as pl
from jax.experimental.pallas import tpu as pltpu
from jax.sharding import PartitionSpec as P


BLK = 128
ROWS = 32
COLS = 16
YS = 8

highest = lax.Precision.HIGHEST
kernel_params = pltpu.CompilerParams(vmem_limit_bytes=16 << 20)


def half_of(row):
    return (row // 8) % 2


def piece_of(row, col):
    d = (col // 2 + 8 - row // 4) % 8
    x = (row // 8 + ((0xEC46 >> (2 * d)) & 3)) % 4
    far = (0x87 >> d) & 1
    near_e = 1 - (row % 4) // 2
    return 2 * x + (near_e + far) % 2


def holder_of(y, q, x):
    return 8 * x + (4 * (y % 2) + 6 + 2 * q) % 8


def spread_pairs():
    pairs = []
    for row in range(ROWS):
        for col in range(COLS):
            t = piece_of(row, col)
            target = holder_of(row // 4, row % 4, t // 2) + t % 2
            pairs.append((row * COLS + col, target * COLS + 2 * (row // 4) + col % 2))
    return pairs


def select_columns(core):
    source = lax.broadcasted_iota(jnp.int32, (512, 256), 0)
    n = lax.broadcasted_iota(jnp.int32, (512, 256), 1)
    wanted = 64 * ((n % 128) // 16) + 32 * core + 16 * (n // 128) + n % 16
    return (source == wanted).astype(jnp.float32)


def dot(left, right):
    return jnp.dot(left, right, precision=highest, preferred_element_type=jnp.float32)


def piece_kernel(slots, panel, prev, out, ids, buffer, rows, sems):
    row = lax.axis_index("prow")
    col = lax.axis_index("pcol")
    piece = piece_of(row, col)
    offset = 32 * (piece % 4)
    copies = [
        pltpu.make_async_copy(panel.at[0, pl.ds(BLK * k + offset, 32), :], buffer.at[k], sems.at[k]) for k in range(2)
    ]
    copies.append(pltpu.make_async_copy(prev.at[0], rows, sems.at[2]))
    copies.append(pltpu.make_async_copy(slots, ids, sems.at[3]))
    for copy in copies:
        copy.start()
    wanted = 2 * row + piece // 4
    columns = select_columns(col % 2)
    for copy in copies:
        copy.wait()
    rolled = pltpu.roll(rows[...], (16 - 4 * (piece // 2)) % 16, 0)
    zero = jnp.zeros((32, 512), jnp.float32)
    chunk = jnp.where(ids[0, 2 * row] == wanted, buffer[0], zero)
    chunk = jnp.where(ids[0, 2 * row + 1] == wanted, buffer[1], chunk)
    out[...] = dot(jnp.concatenate([chunk, rolled[:8]], 0), columns)


def own_piece(slot_blocks, panel_blocks, prev_panel):
    return pl.pallas_call(
        piece_kernel,
        out_shape=jax.ShapeDtypeStruct((40, 256), jnp.float32),
        in_specs=[pl.BlockSpec(memory_space=pltpu.HBM)] * 3,
        out_specs=pl.BlockSpec(memory_space=pltpu.VMEM),
        scratch_shapes=[
            pltpu.SMEM((1, 64), jnp.int32),
            pltpu.VMEM((2, 32, 512), jnp.float32),
            pltpu.VMEM((16, 512), jnp.float32),
            pltpu.SemaphoreType.DMA((4,)),
        ],
        name="own_piece",
    )(slot_blocks, panel_blocks, prev_panel)


def factor_halves(slots, panel, row):
    first, second = panel[0, :BLK, :], panel[0, BLK:, :]
    zero = jnp.zeros_like(first)
    low = jnp.where(slots[0, 2 * row] == 2 * row, first, zero)
    high = jnp.where(slots[0, 2 * row + 1] == 2 * row + 1, second, zero)
    return low, jnp.where(slots[0, 2 * row] == 2 * row + 1, first, high)


def cross_kernel(slots, panel, top_column, top_diag, prev, mine, others):
    row = lax.axis_index("prow")
    core = lax.axis_index("pcol") % 2
    low, high = factor_halves(slots, panel, row)
    diag = pltpu.roll(top_diag[...], (512 - 16 * row) % 512, 1)[:, :16]
    part = dot(top_column[:, :BLK], low) + dot(top_column[:, BLK:], high) + dot(diag, prev[0])
    shifted = jnp.where(core == 0, pltpu.roll(part, 480, 1), pltpu.roll(part, 32, 1))
    both = dot(jnp.concatenate([part, shifted], 0), select_columns(core))
    mine[...] = both[:32]
    others[...] = both[32:]


def cross_rows(slot_blocks, panel_blocks, top_column, top_diag, prev_panel):
    return pl.pallas_call(
        cross_kernel,
        out_shape=(
            jax.ShapeDtypeStruct((32, 256), jnp.float32),
            jax.ShapeDtypeStruct((32, 256), jnp.float32),
        ),
        in_specs=[pl.BlockSpec(memory_space=pltpu.SMEM)] + [pl.BlockSpec(memory_space=pltpu.VMEM)] * 4,
        out_specs=(pl.BlockSpec(memory_space=pltpu.VMEM),) * 2,
        compiler_params=kernel_params,
        name="cross_rows",
    )(slot_blocks, panel_blocks, top_column, top_diag, prev_panel)


def gather_kernel(spread, cross_own, cross_other, prev, out):
    row = lax.axis_index("prow")
    core = lax.axis_index("pcol") % 2
    mine, others = cross_own[...], cross_other[...]
    pair = [jnp.where(core == 0, mine, others), jnp.where(core == 0, others, mine)]
    for k in range(ROWS):
        span = slice(128 * half_of(k), 128 * half_of(k) + 128)
        out[k, :36, :] = spread[:36, span]
        for lane in range(2):
            for who in range(2):
                at = 36 + 2 * who + lane
                out[k, at : at + 1, :] = pair[who][k : k + 1, 128 * lane : 128 * lane + 128]
    for parity in range(2):

        @pl.when(row % 2 == parity)
        def _():
            for k in range(16):
                for lane in range(4):
                    span = slice(128 * lane, 128 * lane + 128)
                    out[16 * parity + k, 32 + lane : 33 + lane, :] = prev[0, k : k + 1, span]


def gather_operand(spread, cross_own, cross_other, prev_panel):
    return pl.pallas_call(
        gather_kernel,
        out_shape=jax.ShapeDtypeStruct((ROWS, 40, 128), jnp.float32),
        in_specs=[pl.BlockSpec(memory_space=pltpu.VMEM)] * 4,
        out_specs=pl.BlockSpec(memory_space=pltpu.VMEM),
        compiler_params=kernel_params,
        name="gather_operand",
    )(spread, cross_own, cross_other, prev_panel)


def product_kernel(got, mine, mine_b, next_x, next_xb, out, cross_pair, stride, prev_rows, pieces):
    row = lax.axis_index("prow")
    core = lax.axis_index("pcol") % 2
    y = lax.axis_index("pcol") // 2
    half = half_of(row)
    strided = row // 16
    for k in range(COLS):
        stride[4 * k : 4 * k + 4, :] = got[2 * k + strided, 32:36, :]
    for q in range(4):
        for x in range(4):
            at = holder_of(y, q, x)
            prev_rows[16 * q + 4 * x : 16 * q + 4 * x + 4, :] = got[at + 1 - strided, 32:36, :]
            pieces[256 * q + 64 * x : 256 * q + 64 * x + 64, :] = got[pl.ds(at, 2), :32, :].reshape(64, 128)
    own = pieces[pl.ds(pl.multiple_of(512 * core, 512), 512), :]
    other = pieces[pl.ds(pl.multiple_of(512 - 512 * core, 512), 512), :]
    own_prev = prev_rows[pl.ds(pl.multiple_of(32 * core, 32), 32), :]
    other_prev = prev_rows[pl.ds(pl.multiple_of(32 - 32 * core, 32), 32), :]
    prev = jnp.concatenate([own_prev, other_prev], 0)
    sums = -jnp.sum(got[:, 32:40, :], 0)
    pad = jnp.zeros((4, 128), jnp.float32)
    cross = jnp.concatenate([sums[4:8], pad], 0)
    cross_pair[...] = cross
    for left, right, which in ((mine, mine_b, half), (next_x, next_xb, 1 - half)):
        top = jnp.concatenate([left[256:, :256], left[256:, 256:], right[256:, :256], right[256:, 256:]], 0)
        part = dot(left[:256, :], own) + dot(right[:256, :], other) + dot(top.T, prev)
        part = part.T
        for k in range(YS):
            out[2 * k + which, :16, :] = part[16 * k : 16 * k + 16, :128]
            out[2 * k + which, 16:32, :] = part[16 * k : 16 * k + 16, 128:]
            out[2 * k + which, 32:, :] = cross


def column_product(got, mine, mine_b, next_x, next_xb):
    return pl.pallas_call(
        product_kernel,
        out_shape=(
            jax.ShapeDtypeStruct((16, 40, 128), jnp.float32),
            jax.ShapeDtypeStruct((8, 128), jnp.float32),
            jax.ShapeDtypeStruct((64, 128), jnp.float32),
        ),
        in_specs=[pl.BlockSpec(memory_space=pltpu.VMEM)] * 5,
        out_specs=(pl.BlockSpec(memory_space=pltpu.VMEM),) * 3,
        scratch_shapes=[pltpu.VMEM((64, 128), jnp.float32), pltpu.VMEM((1024, 128), jnp.float32)],
        compiler_params=kernel_params,
        name="column_product",
    )(got, mine, mine_b, next_x, next_xb)


def diag_kernel(slots, panel, got, cross_pair, stride, fresh_out, out, columns):
    row = lax.axis_index("prow")
    half = half_of(row)
    y = lax.axis_index("pcol") // 2
    fresh = []
    for h in range(2):
        total = got[h, :32, :]
        for k in range(1, YS):
            total = total + got[2 * k + h, :32, :]
        fresh.append(jnp.concatenate([-total[:16], -total[16:]], 1))
    fresh = jnp.concatenate(fresh, 0)
    fresh_out[0] = fresh
    low, high = factor_halves(slots, panel, row)
    part = dot(fresh[:, :BLK], low) + dot(fresh[:, BLK:], high)
    for k in range(YS):
        block = got[2 * k + half, 32:40, :]
        for who in range(2):
            for h in range(2):
                columns[h, 2 * k + who : 2 * k + who + 1, :] = block[2 * who + h : 2 * who + h + 1]
    rows = jnp.concatenate([stride[pl.ds(lane, 16, stride=4), :] for lane in range(4)], 1)
    own = []
    for h in range(2):
        columns[2 + h, :, :] = jnp.zeros((128, 128), jnp.float32)
        columns[2 + h, :, :16] = columns[h, :16, :].T
        picked = columns[2 + h, pl.ds(pl.multiple_of(16 * y, 16), 16), :]
        own.append(dot(picked[:, :16], rows))
    part = part + jnp.concatenate(own, 0)
    for k in range(ROWS):
        for lane in range(4):
            out[k, lane : lane + 1, :] = part[k : k + 1, 128 * lane : 128 * lane + 128]
        out[k, 4:8, :] = cross_pair[:4, :]


def diag_operand(slot_blocks, panel_blocks, got, cross_pair, stride):
    return pl.pallas_call(
        diag_kernel,
        out_shape=(
            jax.ShapeDtypeStruct((1, 32, 256), jnp.float32),
            jax.ShapeDtypeStruct((ROWS, 8, 128), jnp.float32),
        ),
        in_specs=[pl.BlockSpec(memory_space=pltpu.SMEM)] + [pl.BlockSpec(memory_space=pltpu.VMEM)] * 4,
        out_specs=(pl.BlockSpec(memory_space=pltpu.VMEM),) * 2,
        scratch_shapes=[pltpu.VMEM((4, 128, 128), jnp.float32)],
        compiler_params=kernel_params,
        name="diag_operand",
    )(slot_blocks, panel_blocks, got, cross_pair, stride)


def total_kernel(got, out, keep, give):
    core = lax.axis_index("pcol") % 2
    total = jnp.sum(got[:, :4, :], 0)
    for k in range(ROWS):
        out[k] = total
        for lane in range(2):
            span = slice(128 * lane, 128 * lane + 128)
            first, second = got[k, 4 + lane : 5 + lane, :], got[k, 6 + lane : 7 + lane, :]
            keep[k : k + 1, span] = jnp.where(core == 0, first, second)
            give[k : k + 1, span] = jnp.where(core == 0, second, first)


def total_operand(got):
    return pl.pallas_call(
        total_kernel,
        out_shape=(
            jax.ShapeDtypeStruct((ROWS, 4, 128), jnp.float32),
            jax.ShapeDtypeStruct((32, 256), jnp.float32),
            jax.ShapeDtypeStruct((32, 256), jnp.float32),
        ),
        in_specs=[pl.BlockSpec(memory_space=pltpu.VMEM)],
        out_specs=(pl.BlockSpec(memory_space=pltpu.VMEM),) * 3,
        compiler_params=kernel_params,
        name="total_operand",
    )(got)


def place_columns(core):
    n = lax.broadcasted_iota(jnp.int32, (256, 512), 0)
    target = lax.broadcasted_iota(jnp.int32, (256, 512), 1)
    return (target == 64 * ((n % 128) // 16) + 32 * core + 16 * (n // 128) + n % 16).astype(jnp.float32)


def line_kernel(keep, taken, out):
    core = lax.axis_index("pcol") % 2
    out[0] = dot(keep[...], place_columns(core)) + dot(taken[...], place_columns(1 - core))


def cross_lines(keep, taken):
    return pl.pallas_call(
        line_kernel,
        out_shape=jax.ShapeDtypeStruct((1, 32, 512), jnp.float32),
        in_specs=[pl.BlockSpec(memory_space=pltpu.VMEM)] * 2,
        out_specs=pl.BlockSpec(memory_space=pltpu.VMEM),
        compiler_params=kernel_params,
        name="cross_lines",
    )(keep, taken)


def last_kernel(got, pivot, out):
    for k in range(ROWS):
        for lane in range(4):
            span = slice(128 * lane, 128 * lane + 128)
            out[0, k : k + 1, span] = pivot[0, k : k + 1, span] - got[k, lane : lane + 1, :]


def last_step(got, pivot_inverse):
    return pl.pallas_call(
        last_kernel,
        out_shape=jax.ShapeDtypeStruct((1, 32, 512), jnp.float32),
        in_specs=[pl.BlockSpec(memory_space=pltpu.VMEM)] * 2,
        out_specs=pl.BlockSpec(memory_space=pltpu.VMEM),
        compiler_params=kernel_params,
        name="last_step",
    )(got, pivot_inverse)


def step(pool_inverse, panel_blocks, prev_panel, pivot_inverse, top_column, top_diag, slot_blocks):
    core_swap = [(i, i ^ 1) for i in range(COLS)]
    row_swap = [(i, i ^ 8) for i in range(ROWS)]

    sent = own_piece(slot_blocks, panel_blocks, prev_panel)
    sent, top_column = lax.optimization_barrier((sent, top_column))
    spread = lax.ppermute(sent, ("prow", "pcol"), spread_pairs())

    blocks = jnp.concatenate([pool_inverse, jnp.concatenate([top_column[:16], top_column[16:]], 1)], 0)
    blocks_x = lax.ppermute(blocks, "prow", row_swap)
    blocks_b = lax.ppermute(blocks, "pcol", core_swap)

    cross_own, cross_sent = cross_rows(slot_blocks, panel_blocks, top_column, top_diag, prev_panel)
    cross_other = lax.ppermute(cross_sent, "pcol", core_swap)

    send = gather_operand(spread, cross_own, cross_other, prev_panel)
    got = lax.all_to_all(send, "prow", 0, 0, tiled=True)
    blocks_xb = lax.ppermute(blocks_x, "pcol", core_swap)

    send, cross_pair, stride = column_product(got, blocks, blocks_b, blocks_x, blocks_xb)
    groups = [
        [((2 * x + h) * 8 + z) * COLS + 2 * i + k for i in range(YS) for h in range(2)]
        for x in range(2)
        for z in range(8)
        for k in range(2)
    ]
    got = lax.all_to_all(send, ("prow", "pcol"), 0, 0, tiled=True, axis_index_groups=groups)
    fresh, send = diag_operand(slot_blocks, panel_blocks, got, cross_pair, stride)
    got = lax.all_to_all(send, "prow", 0, 0, tiled=True)
    total, keep, give = total_operand(got)
    got = lax.all_to_all(total, "prow", 0, 0, tiled=True)
    taken = lax.ppermute(give, "pcol", core_swap)
    cross_out = cross_lines(keep, taken)
    return fresh, cross_out, last_step(got, pivot_inverse)


def solution(mesh):
    in_specs = (
        P("prow", "pcol"),
        P(None, "prow", None),
        P(None, "prow", None),
        P(None, "pcol", None),
        P("pcol", "prow"),
        P("pcol", None),
        P(),
    )
    out_specs = (P(None, "pcol", "prow"), P(None, "pcol", None), P(None, "pcol", None))
    return jax.shard_map(step, mesh=mesh, in_specs=in_specs, out_specs=out_specs, check_vma=False)
```

```python
import jax
import jax.numpy as jnp
from jax import lax
from jax.experimental import pallas as pl
from jax.experimental.pallas import tpu as pltpu
from jax.sharding import PartitionSpec as P


BLK = 128
ROWS = 32
COLS = 16
YS = 8

highest = lax.Precision.HIGHEST
kernel_params = pltpu.CompilerParams(vmem_limit_bytes=16 << 20)


def half_of(row):
    return (row // 8) % 2


def piece_of(row, col):
    d = (col // 2 + 8 - row // 4) % 8
    x = (row // 8 + ((0xEC46 >> (2 * d)) & 3)) % 4
    far = (0x87 >> d) & 1
    near_e = 1 - (row % 4) // 2
    return 2 * x + (near_e + far) % 2


def holder_of(y, q, x):
    return 8 * x + (4 * (y % 2) + 6 + 2 * q) % 8


def spread_pairs():
    pairs = []
    for row in range(ROWS):
        for col in range(COLS):
            t = piece_of(row, col)
            target = holder_of(row // 4, row % 4, t // 2) + t % 2
            pairs.append((row * COLS + col, target * COLS + 2 * (row // 4) + col % 2))
    return pairs


def select_columns(core):
    source = lax.broadcasted_iota(jnp.int32, (512, 256), 0)
    n = lax.broadcasted_iota(jnp.int32, (512, 256), 1)
    wanted = 64 * ((n % 128) // 16) + 32 * core + 16 * (n // 128) + n % 16
    return (source == wanted).astype(jnp.float32)


def dot(left, right):
    return jnp.dot(left, right, precision=highest, preferred_element_type=jnp.float32)


def piece_kernel(slots, panel, prev, top_diag, out, diag_out, ids, buffer, rows, sems):
    row = lax.axis_index("prow")
    col = lax.axis_index("pcol")
    piece = piece_of(row, col)
    offset = 32 * (piece % 4)
    copies = [
        pltpu.make_async_copy(panel.at[0, pl.ds(BLK * k + offset, 32), :], buffer.at[k], sems.at[k]) for k in range(2)
    ]
    copies.append(pltpu.make_async_copy(prev.at[0], rows, sems.at[2]))
    copies.append(pltpu.make_async_copy(slots, ids, sems.at[3]))
    copies.append(pltpu.make_async_copy(top_diag.at[:, pl.ds(BLK * (row // 8), BLK)], diag_out, sems.at[4]))
    for copy in copies:
        copy.start()
    wanted = 2 * row + piece // 4
    columns = select_columns(col % 2)
    for copy in copies:
        copy.wait()
    rolled = pltpu.roll(rows[...], (16 - 4 * (piece // 2)) % 16, 0)
    zero = jnp.zeros((32, 512), jnp.float32)
    chunk = jnp.where(ids[0, 2 * row] == wanted, buffer[0], zero)
    chunk = jnp.where(ids[0, 2 * row + 1] == wanted, buffer[1], chunk)
    out[...] = dot(jnp.concatenate([chunk, rolled[:8]], 0), columns)


def own_piece(slot_blocks, panel_blocks, prev_panel, top_diag):
    return pl.pallas_call(
        piece_kernel,
        out_shape=(
            jax.ShapeDtypeStruct((40, 256), jnp.float32),
            jax.ShapeDtypeStruct((32, BLK), jnp.float32),
        ),
        in_specs=[pl.BlockSpec(memory_space=pltpu.HBM)] * 4,
        out_specs=(pl.BlockSpec(memory_space=pltpu.VMEM),) * 2,
        scratch_shapes=[
            pltpu.SMEM((1, 64), jnp.int32),
            pltpu.VMEM((2, 32, 512), jnp.float32),
            pltpu.VMEM((16, 512), jnp.float32),
            pltpu.SemaphoreType.DMA((5,)),
        ],
        name="own_piece",
    )(slot_blocks, panel_blocks, prev_panel, top_diag)


def factor_halves(slots, panel, row):
    first, second = panel[0, :BLK, :], panel[0, BLK:, :]
    zero = jnp.zeros_like(first)
    low = jnp.where(slots[0, 2 * row] == 2 * row, first, zero)
    high = jnp.where(slots[0, 2 * row + 1] == 2 * row + 1, second, zero)
    return low, jnp.where(slots[0, 2 * row] == 2 * row + 1, first, high)


def cross_kernel(slots, panel, top_column, top_diag, prev, mine, others):
    row = lax.axis_index("prow")
    core = lax.axis_index("pcol") % 2
    low, high = factor_halves(slots, panel, row)
    diag = pltpu.roll(top_diag[...], (BLK - 16 * (row % 8)) % BLK, 1)[:, :16]
    part = dot(top_column[:, :BLK], low) + dot(top_column[:, BLK:], high) + dot(diag, prev[0])
    shifted = jnp.where(core == 0, pltpu.roll(part, 480, 1), pltpu.roll(part, 32, 1))
    both = dot(jnp.concatenate([part, shifted], 0), select_columns(core))
    mine[...] = both[:32]
    others[...] = both[32:]


def cross_rows(slot_blocks, panel_blocks, top_column, top_diag, prev_panel):
    return pl.pallas_call(
        cross_kernel,
        out_shape=(
            jax.ShapeDtypeStruct((32, 256), jnp.float32),
            jax.ShapeDtypeStruct((32, 256), jnp.float32),
        ),
        in_specs=[pl.BlockSpec(memory_space=pltpu.SMEM)] + [pl.BlockSpec(memory_space=pltpu.VMEM)] * 4,
        out_specs=(pl.BlockSpec(memory_space=pltpu.VMEM),) * 2,
        compiler_params=kernel_params,
        name="cross_rows",
    )(slot_blocks, panel_blocks, top_column, top_diag, prev_panel)


def gather_kernel(spread, cross_own, cross_other, prev, out):
    row = lax.axis_index("prow")
    core = lax.axis_index("pcol") % 2
    mine, others = cross_own[...], cross_other[...]
    pair = [jnp.where(core == 0, mine, others), jnp.where(core == 0, others, mine)]
    for k in range(ROWS):
        span = slice(128 * half_of(k), 128 * half_of(k) + 128)
        out[k, :36, :] = spread[:36, span]
        for lane in range(2):
            for who in range(2):
                at = 36 + 2 * who + lane
                out[k, at : at + 1, :] = pair[who][k : k + 1, 128 * lane : 128 * lane + 128]
    for parity in range(2):

        @pl.when(row % 2 == parity)
        def _():
            for k in range(16):
                for lane in range(4):
                    span = slice(128 * lane, 128 * lane + 128)
                    out[16 * parity + k, 32 + lane : 33 + lane, :] = prev[0, k : k + 1, span]


def gather_operand(spread, cross_own, cross_other, prev_panel):
    return pl.pallas_call(
        gather_kernel,
        out_shape=jax.ShapeDtypeStruct((ROWS, 40, 128), jnp.float32),
        in_specs=[pl.BlockSpec(memory_space=pltpu.VMEM)] * 4,
        out_specs=pl.BlockSpec(memory_space=pltpu.VMEM),
        compiler_params=kernel_params,
        name="gather_operand",
    )(spread, cross_own, cross_other, prev_panel)


def product_kernel(got, mine, mine_b, next_x, next_xb, out, cross_pair, stride, prev_rows, pieces):
    row = lax.axis_index("prow")
    core = lax.axis_index("pcol") % 2
    y = lax.axis_index("pcol") // 2
    half = half_of(row)
    strided = row // 16
    for k in range(COLS):
        stride[4 * k : 4 * k + 4, :] = got[2 * k + strided, 32:36, :]
    for q in range(4):
        for x in range(4):
            at = holder_of(y, q, x)
            prev_rows[16 * q + 4 * x : 16 * q + 4 * x + 4, :] = got[at + 1 - strided, 32:36, :]
            pieces[256 * q + 64 * x : 256 * q + 64 * x + 64, :] = got[pl.ds(at, 2), :32, :].reshape(64, 128)
    own = pieces[pl.ds(pl.multiple_of(512 * core, 512), 512), :]
    other = pieces[pl.ds(pl.multiple_of(512 - 512 * core, 512), 512), :]
    own_prev = prev_rows[pl.ds(pl.multiple_of(32 * core, 32), 32), :]
    other_prev = prev_rows[pl.ds(pl.multiple_of(32 - 32 * core, 32), 32), :]
    prev = jnp.concatenate([own_prev, other_prev], 0)
    sums = -jnp.sum(got[:, 32:40, :], 0)
    pad = jnp.zeros((4, 128), jnp.float32)
    cross = jnp.concatenate([sums[4:8], pad], 0)
    cross_pair[...] = cross
    for left, right, which in ((mine, mine_b, half), (next_x, next_xb, 1 - half)):
        top = jnp.concatenate([left[256:, :256], left[256:, 256:], right[256:, :256], right[256:, 256:]], 0)
        part = dot(left[:256, :], own) + dot(right[:256, :], other) + dot(top.T, prev)
        part = part.T
        for k in range(YS):
            out[2 * k + which, :16, :] = part[16 * k : 16 * k + 16, :128]
            out[2 * k + which, 16:32, :] = part[16 * k : 16 * k + 16, 128:]
            out[2 * k + which, 32:, :] = cross


def column_product(got, mine, mine_b, next_x, next_xb):
    return pl.pallas_call(
        product_kernel,
        out_shape=(
            jax.ShapeDtypeStruct((16, 40, 128), jnp.float32),
            jax.ShapeDtypeStruct((8, 128), jnp.float32),
            jax.ShapeDtypeStruct((64, 128), jnp.float32),
        ),
        in_specs=[pl.BlockSpec(memory_space=pltpu.VMEM)] * 5,
        out_specs=(pl.BlockSpec(memory_space=pltpu.VMEM),) * 3,
        scratch_shapes=[pltpu.VMEM((64, 128), jnp.float32), pltpu.VMEM((1024, 128), jnp.float32)],
        compiler_params=kernel_params,
        name="column_product",
    )(got, mine, mine_b, next_x, next_xb)


def diag_kernel(slots, panel, got, cross_pair, stride, fresh_out, out, columns):
    row = lax.axis_index("prow")
    half = half_of(row)
    y = lax.axis_index("pcol") // 2
    fresh = []
    for h in range(2):
        total = got[h, :32, :]
        for k in range(1, YS):
            total = total + got[2 * k + h, :32, :]
        fresh.append(jnp.concatenate([-total[:16], -total[16:]], 1))
    fresh = jnp.concatenate(fresh, 0)
    fresh_out[0] = fresh
    low, high = factor_halves(slots, panel, row)
    part = dot(fresh[:, :BLK], low) + dot(fresh[:, BLK:], high)
    for k in range(YS):
        block = got[2 * k + half, 32:40, :]
        for who in range(2):
            for h in range(2):
                columns[h, 2 * k + who : 2 * k + who + 1, :] = block[2 * who + h : 2 * who + h + 1]
    rows = jnp.concatenate([stride[pl.ds(lane, 16, stride=4), :] for lane in range(4)], 1)
    own = []
    for h in range(2):
        columns[2 + h, :, :] = jnp.zeros((128, 128), jnp.float32)
        columns[2 + h, :, :16] = columns[h, :16, :].T
        picked = columns[2 + h, pl.ds(pl.multiple_of(16 * y, 16), 16), :]
        own.append(dot(picked[:, :16], rows))
    part = part + jnp.concatenate(own, 0)
    for k in range(ROWS):
        for lane in range(4):
            out[k, lane : lane + 1, :] = part[k : k + 1, 128 * lane : 128 * lane + 128]
        out[k, 4:8, :] = cross_pair[:4, :]


def diag_operand(slot_blocks, panel_blocks, got, cross_pair, stride):
    return pl.pallas_call(
        diag_kernel,
        out_shape=(
            jax.ShapeDtypeStruct((1, 32, 256), jnp.float32),
            jax.ShapeDtypeStruct((ROWS, 8, 128), jnp.float32),
        ),
        in_specs=[pl.BlockSpec(memory_space=pltpu.SMEM)] + [pl.BlockSpec(memory_space=pltpu.VMEM)] * 4,
        out_specs=(pl.BlockSpec(memory_space=pltpu.VMEM),) * 2,
        scratch_shapes=[pltpu.VMEM((4, 128, 128), jnp.float32)],
        compiler_params=kernel_params,
        name="diag_operand",
    )(slot_blocks, panel_blocks, got, cross_pair, stride)


def total_kernel(got, out, keep, give):
    core = lax.axis_index("pcol") % 2
    total = jnp.sum(got[:, :4, :], 0)
    for k in range(ROWS):
        out[k] = total
        for lane in range(2):
            span = slice(128 * lane, 128 * lane + 128)
            first, second = got[k, 4 + lane : 5 + lane, :], got[k, 6 + lane : 7 + lane, :]
            keep[k : k + 1, span] = jnp.where(core == 0, first, second)
            give[k : k + 1, span] = jnp.where(core == 0, second, first)


def total_operand(got):
    return pl.pallas_call(
        total_kernel,
        out_shape=(
            jax.ShapeDtypeStruct((ROWS, 4, 128), jnp.float32),
            jax.ShapeDtypeStruct((32, 256), jnp.float32),
            jax.ShapeDtypeStruct((32, 256), jnp.float32),
        ),
        in_specs=[pl.BlockSpec(memory_space=pltpu.VMEM)],
        out_specs=(pl.BlockSpec(memory_space=pltpu.VMEM),) * 3,
        compiler_params=kernel_params,
        name="total_operand",
    )(got)


def place_columns(core):
    n = lax.broadcasted_iota(jnp.int32, (256, 512), 0)
    target = lax.broadcasted_iota(jnp.int32, (256, 512), 1)
    return (target == 64 * ((n % 128) // 16) + 32 * core + 16 * (n // 128) + n % 16).astype(jnp.float32)


def line_kernel(keep, taken, out):
    core = lax.axis_index("pcol") % 2
    out[0] = dot(keep[...], place_columns(core)) + dot(taken[...], place_columns(1 - core))


def cross_lines(keep, taken):
    return pl.pallas_call(
        line_kernel,
        out_shape=jax.ShapeDtypeStruct((1, 32, 512), jnp.float32),
        in_specs=[pl.BlockSpec(memory_space=pltpu.VMEM)] * 2,
        out_specs=pl.BlockSpec(memory_space=pltpu.VMEM),
        compiler_params=kernel_params,
        name="cross_lines",
    )(keep, taken)


def last_kernel(got, pivot, out):
    for k in range(ROWS):
        for lane in range(4):
            span = slice(128 * lane, 128 * lane + 128)
            out[0, k : k + 1, span] = pivot[0, k : k + 1, span] - got[k, lane : lane + 1, :]


def last_step(got, pivot_inverse):
    return pl.pallas_call(
        last_kernel,
        out_shape=jax.ShapeDtypeStruct((1, 32, 512), jnp.float32),
        in_specs=[pl.BlockSpec(memory_space=pltpu.VMEM)] * 2,
        out_specs=pl.BlockSpec(memory_space=pltpu.VMEM),
        compiler_params=kernel_params,
        name="last_step",
    )(got, pivot_inverse)


def step(pool_inverse, panel_blocks, prev_panel, pivot_inverse, top_column, top_diag, slot_blocks):
    core_swap = [(i, i ^ 1) for i in range(COLS)]
    row_swap = [(i, i ^ 8) for i in range(ROWS)]

    sent, diag_slice = own_piece(slot_blocks, panel_blocks, prev_panel, top_diag)
    sent, top_column = lax.optimization_barrier((sent, top_column))
    spread = lax.ppermute(sent, ("prow", "pcol"), spread_pairs())

    blocks = jnp.concatenate([pool_inverse, jnp.concatenate([top_column[:16], top_column[16:]], 1)], 0)
    blocks_x = lax.ppermute(blocks, "prow", row_swap)
    blocks_b = lax.ppermute(blocks, "pcol", core_swap)

    cross_own, cross_sent = cross_rows(slot_blocks, panel_blocks, top_column, diag_slice, prev_panel)
    cross_other = lax.ppermute(cross_sent, "pcol", core_swap)

    send = gather_operand(spread, cross_own, cross_other, prev_panel)
    got = lax.all_to_all(send, "prow", 0, 0, tiled=True)
    blocks_xb = lax.ppermute(blocks_x, "pcol", core_swap)

    send, cross_pair, stride = column_product(got, blocks, blocks_b, blocks_x, blocks_xb)
    groups = [
        [((2 * x + h) * 8 + z) * COLS + 2 * i + k for i in range(YS) for h in range(2)]
        for x in range(2)
        for z in range(8)
        for k in range(2)
    ]
    got = lax.all_to_all(send, ("prow", "pcol"), 0, 0, tiled=True, axis_index_groups=groups)
    fresh, send = diag_operand(slot_blocks, panel_blocks, got, cross_pair, stride)
    got = lax.all_to_all(send, "prow", 0, 0, tiled=True)
    total, keep, give = total_operand(got)
    got = lax.all_to_all(total, "prow", 0, 0, tiled=True)
    taken = lax.ppermute(give, "pcol", core_swap)
    cross_out = cross_lines(keep, taken)
    return fresh, cross_out, last_step(got, pivot_inverse)


def solution(mesh):
    in_specs = (
        P("prow", "pcol"),
        P(None, "prow", None),
        P(None, "prow", None),
        P(None, "pcol", None),
        P("pcol", "prow"),
        P("pcol", None),
        P(),
    )
    out_specs = (P(None, "pcol", "prow"), P(None, "pcol", None), P(None, "pcol", None))
    return jax.shard_map(step, mesh=mesh, in_specs=in_specs, out_specs=out_specs, check_vma=False)
```
